32 devices in a mesh: dp: 8 (over z, x), state: 4 (over y, core).
Axes of the slice: x: 2, y: 2, z: 4, core: 2. Of those that a mesh axis runs over, the one named last changes fastest.
Arguments:
- block_input: bfloat16 [8192, 2048], P(('dp', 'state')), may hold values from -6 to 6
- width_index: int32 [8], P('dp'), may hold values from 0 to 3
- w_in: bfloat16 [2048, 8512], P('dp', 'state'), may hold values from -0.125 to 0.125
- w_out: bfloat16 [4096, 2048], P('state', 'dp'), may hold values from -0.1875 to 0.1875
- conv_weight: float32 [4, 4352], replicated, may hold values from -3 to 3
- conv_bias: float32 [4352], replicated, may hold values from -2 to 2
- dt_bias: float32 [64], replicated, may hold values from -7 to -3.5
- a_log: float32 [64], replicated, may hold values from 0 to 0.7
- d_skip: float32 [64], replicated, may hold values from 0.5 to 1.5
- norm_in_gain: float32 [2048], replicated, may hold values from 0.5 to 1.5
- norm_out_gain: float32 [4096], replicated, may hold values from 0.5 to 1.5
- out_cotangent: bfloat16 [8192, 2048], P(('dp', 'state')), may hold values from -6 to 6
Outputs:
- block_out: bfloat16 [8192, 2048], P(('dp', 'state'))
- grad_input: float32 [8192, 2048], P(('dp', 'state'))
- grad_in_proj: float32 [2048, 8512], P('dp', 'state')
- grad_out_proj: float32 [4096, 2048], P('state', 'dp')
- grad_conv_weight: float32 [4, 4352], replicated
- grad_conv_bias: float32 [4352], replicated
- grad_dt_bias: float32 [64], replicated
- grad_a_log: float32 [64], replicated
- grad_d_skip: float32 [64], replicated
- grad_norm_in: float32 [2048], replicated
- grad_norm_out: float32 [4096], replicated
The draws below stay inside these ranges and needn't reach their ends.
Inputs may be any that keep to these rules, and one draw needn't show every extreme that they name: `width_index`: a sequence of level w uses the first 64 / 8 * 2^w heads.
All inputs are finite; a program needn't handle non-finite values.
Results may differ from the reference program's by a relative error of at most 0.015.
Values may be sent and summed in bfloat16 or wider, within the bound.
No kernel may reach another device: no remote copies, remote signals or barrier semaphores. Data moves between devices by JAX's collectives and lax.ppermute only.
A program may use at most 192 MiB of HBM per device.

```python
import jax
import jax.numpy as jnp
from jax import lax

D = 2048
H = 64
P_SIZE = 64
N = 128
SPAN = 256
CONV = 4
E = 4096
XBC = 4352
F = 8512
SEQ = 1024
NC = 4
TOKENS = 8192
N_DP = 8


def touch_ends(entries, own_key, least, largest):
    longest = entries.shape.index(max(entries.shape))
    spots = []
    for shift in (0, 1):
        where = [jax.random.randint(jax.random.fold_in(own_key, axis), (), 0, length) for axis, length in enumerate(entries.shape)]
        where[longest] = (where[longest] + shift) % entries.shape[longest]
        spots.append(tuple(where))
    return entries.at[spots[0]].set(least).at[spots[1]].set(largest)


def shard_levels(rng, dims, pieces, least, high):
    gain = 1.0
    for position, shards_of in pieces:
        steps = jax.random.uniform(jax.random.fold_in(jax.random.fold_in(rng, 6), position), (shards_of,), jnp.float32, least / len(pieces), high / len(pieces))
        gain = gain * jnp.repeat(jnp.exp(steps), dims[position] // shards_of).reshape((-1,) + (1,) * (len(dims) - 1 - position))
    return gain


def gaussian(own_key, shape, deviation, reach, cuts=(), kind=jnp.bfloat16):
    array = jax.random.normal(own_key, shape, jnp.float32) * deviation
    if len(cuts) > 0:
        array = shard_levels(own_key, shape, cuts, -0.22, 0.18) * array
    return jnp.clip(array, min=-reach, max=reach).astype(kind)


def setup_inputs(seed: int = 0) -> dict:
    keys = jax.random.split(jax.random.key(seed), 13)
    return {
        "block_input": gaussian(keys[0], (TOKENS, D), 1.0, 6.0, ((0, 32),)),
        "width_index": touch_ends(jax.random.randint(keys[1], (N_DP,), 0, 4), jax.random.fold_in(keys[1], 1), 0, 3).astype(jnp.int32),
        "w_in": gaussian(keys[2], (D, F), D ** -0.5, 0.125, ((0, 8), (1, 4))),
        "w_out": gaussian(keys[3], (E, D), (E // 4) ** -0.5, 0.1875, ((0, 4), (1, 8))),
        "conv_weight": gaussian(keys[4], (CONV, XBC), 0.5, 3.0, (), jnp.float32),
        "conv_bias": gaussian(keys[5], (XBC,), 0.3, 2.0, (), jnp.float32),
        "dt_bias": jnp.clip(jax.random.uniform(keys[6], (H,), jnp.float32, -7.0, -3.5), -7.0, -3.5),
        "a_log": jnp.clip(jax.random.uniform(keys[7], (H,), jnp.float32, 0.0, 0.7), 0.0, 0.7),
        "d_skip": jnp.clip(jax.random.uniform(keys[8], (H,), jnp.float32, 0.5, 1.5), 0.5, 1.5),
        "norm_in_gain": jnp.clip(1.0 + 0.1 * jax.random.normal(keys[9], (D,), jnp.float32), 0.5, 1.5),
        "norm_out_gain": jnp.clip(1.0 + 0.1 * jax.random.normal(keys[10], (E,), jnp.float32), 0.5, 1.5),
        "out_cotangent": gaussian(keys[11], (TOKENS, D), 1.0, 6.0, ((0, 32),)),
    }


EPSILON = 1e-05
HIGHEST = lax.Precision.HIGHEST

@jax.custom_vjp
def low(v):
    return lax.optimization_barrier(v.astype(jnp.bfloat16)).astype(jnp.float32)

@jax.custom_vjp
def low_back(v):
    return v

def low_keep(v):
    return (low(v), None)

def low_pass(kept, grad):
    return (grad,)

def back_keep(v):
    return (v, None)

def back_low(kept, grad):
    return (low(grad),)
low.defvjp(low_keep, low_pass)
low_back.defvjp(back_keep, back_low)

def norm_rows(values, norm_gain):
    return values * lax.rsqrt(lax.optimization_barrier(jnp.mean(values * values, axis=-1, keepdims=True)) + EPSILON) * norm_gain

def gate_norm(mixed_in, gate_in, norm_gain, channel_mask, active_count):
    gated = mixed_in * jax.nn.silu(gate_in)
    mean_square = lax.optimization_barrier(jnp.sum(channel_mask * gated * gated, axis=-1, keepdims=True)) / active_count
    return gated * lax.rsqrt(mean_square + EPSILON) * norm_gain * channel_mask

def seq_forward(params, tokens, width_level):
    w_in, w_out, conv_weight, conv_bias, dt_bias, a_log, d_skip, gain_in, gain_out = params
    normed = low(norm_rows(tokens, gain_in))
    projected = low_back(low(jnp.dot(normed, w_in, precision=HIGHEST)))
    gate_part = projected[:, :E]
    inner_part = projected[:, E:E + XBC]
    dt_raw = projected[:, E + XBC:]
    padded = jnp.pad(inner_part, ((CONV - 1, 0), (0, 0)))
    convolved = conv_bias + jnp.zeros((SEQ, XBC), jnp.float32)
    for offset in range(CONV):
        convolved = convolved + conv_weight[offset] * padded[offset:offset + SEQ]
    activated = jax.nn.silu(convolved)
    values = low(activated[:, :E]).reshape(NC, SPAN, H, P_SIZE)
    inputs_b = low(activated[:, E:E + N]).reshape(NC, SPAN, N)
    readout = low(activated[:, E + N:]).reshape(NC, SPAN, N)
    step_size = jax.nn.softplus(dt_raw + dt_bias).reshape(NC, SPAN, H)
    decay_rate = -jnp.exp(a_log)
    log_decay = jnp.cumsum(step_size * decay_rate, axis=1)
    scores = low_back(jnp.einsum('kqn,ksn->kqs', readout, inputs_b, precision=HIGHEST))
    causal_mask = jnp.arange(SPAN)[:, None] >= jnp.arange(SPAN)[None, :]
    by_head = jnp.transpose(log_decay, (0, 2, 1))
    decay_table = jnp.exp(jnp.where(causal_mask, by_head[:, :, :, None] - by_head[:, :, None, :], -jnp.inf))
    step_by_head = jnp.transpose(step_size, (0, 2, 1))
    mix_weights = low(scores[:, None] * decay_table * step_by_head[:, :, None, :])
    inner_out = jnp.einsum('khqs,kshp->kqhp', mix_weights, values, precision=HIGHEST)
    tail_weight = jnp.exp(log_decay[:, -1:, :] - log_decay) * step_size
    weighted = low(values * tail_weight[..., None])
    span_states = low_back(jnp.einsum('kshp,ksn->khpn', weighted, inputs_b, precision=HIGHEST))
    totals = log_decay[:, -1, :]

    @jax.checkpoint
    def advance(carried, scanned):
        state_in, span_total = scanned
        return (jnp.exp(span_total)[:, None, None] * carried + state_in, carried)
    _, starts = lax.scan(advance, jnp.zeros((H, P_SIZE, N), jnp.float32), (span_states, totals))
    carried_out = low_back(jnp.einsum('kqn,khpn->kqhp', readout, low(starts), precision=HIGHEST))
    mixed = low_back(inner_out + jnp.exp(log_decay)[..., None] * carried_out + d_skip[:, None] * values)
    heads_on = H // 8 * jnp.left_shift(1, width_level)
    channel_mask = (jnp.arange(E) // P_SIZE < heads_on).astype(jnp.float32)
    active_count = (heads_on * P_SIZE).astype(jnp.float32)
    normed_out = low(gate_norm(mixed.reshape(SEQ, E), gate_part, gain_out, channel_mask, active_count))
    return tokens + jnp.dot(normed_out, w_out, precision=HIGHEST)

def reference(block_input, width_index, w_in, w_out, conv_weight, conv_bias, dt_bias, a_log, d_skip, norm_in_gain, norm_out_gain, out_cotangent):
    params = tuple((item.astype(jnp.float32) for item in (w_in, w_out, conv_weight, conv_bias, dt_bias, a_log, d_skip, norm_in_gain, norm_out_gain)))
    inputs = block_input.astype(jnp.float32).reshape(N_DP, SEQ, D)
    cotangents = out_cotangent.astype(jnp.float32).reshape(N_DP, SEQ, D)
    zeros = jax.tree.map(jnp.zeros_like, params)

    def one_sequence(accum, scanned):
        tokens, cotangent, width_level = scanned

        def forward(params_in, tokens_in):
            return seq_forward(params_in, tokens_in, width_level)
        result, pull = jax.vjp(forward, params, tokens)
        param_grads, token_grads = pull(cotangent)
        accum = jax.tree.map(lambda left, right: left + right, accum, param_grads)
        return (accum, (result.astype(jnp.bfloat16), token_grads))
    accum, (results, token_grads) = lax.scan(one_sequence, zeros, (inputs, cotangents, width_index))
    return (results.reshape(TOKENS, D), token_grads.reshape(TOKENS, D), accum[0], accum[1], accum[2], accum[3], accum[4], accum[5], accum[6], accum[7], accum[8])
```

```python
import jax
import jax.numpy as jnp
from jax import lax
from jax.sharding import PartitionSpec as P

H = 64
P_SIZE = 64
N = 128
SPAN = 256
CONV = 4
EPSILON = 1e-05
F32 = jnp.float32
BF16 = jnp.bfloat16


def mm(left, right, dims):
    return lax.dot_general(left, right, (dims, ((), ())), preferred_element_type=F32)


def flip(value, axis, bit):
    count = lax.axis_size(axis)
    return lax.ppermute(value, axis, [(i, i ^ bit) for i in range(count)])


def window(piece, piece_start, start, width):
    have = piece.shape[1]
    padded = jnp.pad(piece, ((0, 0), (width, width)))
    offset = jnp.clip(start - piece_start + width, 0, have + width)
    return lax.dynamic_slice_in_dim(padded, offset, width, 1)


def moves(count, from_range, to_range):
    found = {}
    for source in range(count):
        for target in range(count):
            a, b = from_range(source), to_range(target)
            if source != target and max(a[0], b[0]) < min(a[1], b[1]):
                found.setdefault(target - source, []).append((source, target))
    return found


def gather_state(own):
    count, here = lax.axis_size("state"), lax.axis_index("state")
    out = jnp.zeros((count,) + own.shape, own.dtype)
    held = {0: own}
    bit = count // 2
    while bit:
        for key in list(held):
            held[key | bit] = flip(held[key], "state", bit)
        bit //= 2
    for key, part in held.items():
        out = lax.dynamic_update_index_in_dim(out, part, here ^ key, 0)
    return out


def slots(axis):
    count = lax.axis_size(axis)
    return [(step, other) for step in range(count // 2) for other in range(2)]


def ringed(axis):
    return lax.axis_size(axis) <= 8


def reorder(value, axis):
    if not ringed(axis):
        return value
    count, here = lax.axis_size(axis), lax.axis_index(axis)
    steps = count // 2
    rows, width = value.shape
    pieces = [value[:, i * (width // steps) : (i + 1) * (width // steps)] for i in range(steps)][::-1]
    pair = width // count
    turned = jnp.concatenate(pieces + pieces[:-1], axis=1)
    turned = lax.dynamic_slice_in_dim(turned, (steps - 1 - here // 2) * 2 * pair, width, 1)
    halves = [turned[:, i * pair : (i + 1) * pair] for i in range(count)]
    swapped = jnp.concatenate([halves[i ^ 1] for i in range(count)], axis=1)
    return jnp.where(here % 2 == 0, turned, swapped)


def gather_dp(own):
    count = lax.axis_size("dp")
    if not ringed("dp"):
        every = lax.all_gather(own, "dp")
        return [every[i] for i in range(count)]
    ring = [(i, (i + 2) % count) for i in range(count)]
    out = []
    held = own
    for step in range(count // 2):
        out += [held, flip(held, "dp", 1)]
        if step + 1 < count // 2:
            held = lax.ppermute(held, "dp", ring)
    return out


def scatter_dp(part_of):
    count = lax.axis_size("dp")
    if not ringed("dp"):
        parts = jnp.stack([part_of(i) for i in range(count)])
        return lax.psum_scatter(parts, "dp", scatter_dimension=0, tiled=False)
    ring = [(i, (i + 2) % count) for i in range(count)]
    carried = None
    for step in range(1, count // 2 + 1):
        at = 2 * (step % (count // 2))
        total = part_of(at) + flip(part_of(at + 1).astype(BF16), "dp", 1).astype(F32)
        if carried is not None:
            total = total + carried.astype(F32)
        if step < count // 2:
            carried = lax.ppermute(total.astype(BF16), "dp", ring)
    return total


def scatter_state(part_of):
    count, here = lax.axis_size("state"), lax.axis_index("state")

    order = []
    bit = 1
    while bit < count:
        order.append(bit)
        bit *= 2
    parts = {key: part_of(here ^ key) for key in range(count)}
    for bit in order:
        for key in [k for k in parts if not k & bit]:
            sent = flip(parts.pop(key | bit).astype(BF16), "state", bit)
            parts[key] = parts[key] + sent.astype(F32)
    return parts[0]


def sum_axis(value, axis):
    bit = 1
    while bit < lax.axis_size(axis):
        value = value + flip(value, axis, bit)
        bit *= 2
    return value


def local(
    block_input,
    width_index,
    w_in,
    w_out,
    conv_weight,
    conv_bias,
    dt_bias,
    a_log,
    d_skip,
    norm_in_gain,
    norm_out_gain,
    out_cotangent,
):
    tok_rows, width = block_input.shape
    inner = H * P_SIZE
    xbc = inner + 2 * N
    full_cols = 2 * inner + 2 * N + H
    groups, group = lax.axis_size("state"), lax.axis_index("state")
    seq_rows = tok_rows * groups
    blocks = seq_rows // SPAN
    heads = H // groups
    cols = inner // groups
    store = full_cols // groups
    in_rows = w_in.shape[0]
    tail = 2 * N + H

    def store_range(i):
        return (store * i, store * (i + 1))

    def value_range(i):
        return (inner + cols * i, inner + cols * (i + 1))

    def gate_range(i):
        return (cols * i, cols * (i + 1))

    def tail_range(i):
        return (inner + inner, full_cols)

    def from_store(wanted):
        size = wanted(0)[1] - wanted(0)[0]
        total = window(w_in, store * group, wanted(group)[0], size)
        for shift, pairs in moves(groups, store_range, wanted).items():
            sent = window(w_in, store * group, wanted(group + shift)[0], size)
            total = total + lax.ppermute(sent, "state", pairs)
        return total

    def to_store(piece, held):
        piece = piece.astype(BF16)
        total = window(piece, held(group)[0], store * group, store).astype(F32)
        for shift, pairs in moves(groups, held, store_range).items():
            came = lax.ppermute(piece, "state", pairs)
            total = total + window(came, held(group - shift)[0], store * group, store).astype(F32)
        return total

    tokens = block_input.astype(F32)
    in_scale = lax.rsqrt(jnp.mean(tokens * tokens, axis=-1, keepdims=True) + EPSILON)
    normed = (tokens * in_scale * norm_in_gain).astype(BF16)

    w_x_own = jnp.concatenate([from_store(value_range), from_store(tail_range)], axis=1)
    w_x = jnp.concatenate(gather_dp(w_x_own), axis=0)
    normed_all = gather_state(reorder(normed, "dp")).reshape(seq_rows, width)
    w_g = jnp.concatenate(gather_dp(from_store(gate_range)), axis=0)
    w_o = jnp.concatenate(gather_dp(w_out), axis=1)
    cot_all = gather_state(reorder(out_cotangent, "dp")).reshape(seq_rows, width)

    x_proj = mm(normed_all, w_x, ((1,), (0,))).astype(BF16)
    in_float = x_proj[:, : cols + 2 * N].astype(F32)
    taps = jnp.concatenate(
        [lax.dynamic_slice_in_dim(conv_weight, cols * group, cols, 1), conv_weight[:, inner:]], axis=1
    )
    bias = jnp.concatenate(
        [lax.dynamic_slice_in_dim(conv_bias, cols * group, cols, 0), conv_bias[inner:]], axis=0
    )
    padded = jnp.pad(in_float, ((CONV - 1, 0), (0, 0)))
    convolved = bias + taps[0] * padded[:seq_rows]
    for offset in range(1, CONV):
        convolved = convolved + taps[offset] * padded[offset : offset + seq_rows]
    activated = jax.nn.silu(convolved).astype(BF16)
    values_b = activated[:, :cols].reshape(blocks, SPAN, heads, P_SIZE)
    inputs_b = activated[:, cols : cols + N].reshape(blocks, SPAN, N)
    readout = activated[:, cols + N :].reshape(blocks, SPAN, N)
    values_f = values_b.astype(F32)
    own_heads = heads * group
    dt_raw = lax.dynamic_slice_in_dim(x_proj[:, cols + 2 * N :], own_heads, heads, 1).astype(F32)
    dt_bias_own = lax.dynamic_slice_in_dim(dt_bias, own_heads, heads, 0)
    a_log_own = lax.dynamic_slice_in_dim(a_log, own_heads, heads, 0)
    skip_own = lax.dynamic_slice_in_dim(d_skip, own_heads, heads, 0)
    gain_own = lax.dynamic_slice_in_dim(norm_out_gain, cols * group, cols, 0)

    pre_act = dt_raw + dt_bias_own
    step_size = jax.nn.softplus(pre_act).reshape(blocks, SPAN, heads)
    decay_rate = -jnp.exp(a_log_own)
    log_decay = jnp.cumsum(step_size * decay_rate, axis=1)
    scores = jnp.einsum("kqn,ksn->kqs", readout, inputs_b, preferred_element_type=F32)
    causal_mask = jnp.arange(SPAN)[:, None] >= jnp.arange(SPAN)[None, :]
    by_head = jnp.transpose(log_decay, (0, 2, 1))
    decay_table = jnp.exp(
        jnp.where(causal_mask, by_head[:, :, :, None] - by_head[:, :, None, :], -jnp.inf)
    )
    step_by_head = jnp.transpose(step_size, (0, 2, 1))
    mix_full = scores[:, None] * decay_table * step_by_head[:, :, None, :]
    mix_weights = mix_full.astype(BF16)
    inner_out = jnp.einsum("khqs,kshp->kqhp", mix_weights, values_b, preferred_element_type=F32)
    tail_exp = jnp.exp(log_decay[:, -1:, :] - log_decay)
    tail_weight = tail_exp * step_size
    weighted = (values_f * tail_weight[..., None]).astype(BF16)
    span_states = jnp.einsum("kshp,ksn->khpn", weighted, inputs_b, preferred_element_type=F32)
    totals = log_decay[:, -1, :]
    total_exp = jnp.exp(totals)
    starts = [jnp.zeros((heads, P_SIZE, N), F32)]
    for k in range(blocks - 1):
        starts.append(total_exp[k][:, None, None] * starts[k] + span_states[k])
    starts = jnp.stack(starts)
    starts_low = starts.astype(BF16)
    carried_out = jnp.einsum("kqn,khpn->kqhp", readout, starts_low, preferred_element_type=F32)
    growth = jnp.exp(log_decay)[..., None]
    outer_out = growth * carried_out
    mixed = (inner_out + outer_out + skip_own[:, None] * values_f).reshape(seq_rows, cols)

    gate_part = mm(normed_all, w_g, ((1,), (0,))).astype(BF16).astype(F32)
    out_grad = mm(cot_all, w_o, ((1,), (1,)))
    heads_on = H // 8 * jnp.left_shift(1, width_index[0])
    mask = ((cols * group + jnp.arange(cols)) // P_SIZE < heads_on).astype(F32)
    active = (heads_on * P_SIZE).astype(F32)
    gate_sig = jax.nn.sigmoid(gate_part)
    gate_act = gate_part * gate_sig
    gated = mixed * gate_act
    weighted_grad_out = out_grad * (gain_own * mask)
    stats = jnp.stack(
        [jnp.sum(mask * gated * gated, axis=-1), jnp.sum(weighted_grad_out * gated, axis=-1)]
    )
    stats = lax.psum(stats, "state")
    out_scale = lax.rsqrt(stats[0] / active + EPSILON)[:, None]
    pull = (stats[1] / active)[:, None] * out_scale * out_scale * out_scale
    normed_out = (gated * out_scale * (gain_own * mask)).astype(BF16)
    grad_norm_out = jnp.sum(out_grad * mask * gated * out_scale, axis=0)
    gated_grad = weighted_grad_out * out_scale - gated * mask * pull
    mixed_grad = gated_grad * gate_act
    gate_grad = (gated_grad * mixed * (gate_sig * (1.0 + gate_part * (1.0 - gate_sig)))).astype(BF16)

    rows_of = normed_out.reshape(groups, tok_rows, cols)

    def out_part(i):
        rows = lax.dynamic_index_in_dim(rows_of, i, 0, keepdims=False)
        return mm(rows, w_o, ((1,), (0,)))

    block_out = (tokens + reorder(scatter_state(out_part), "dp")).astype(BF16)

    def grad_out_part(i):
        return mm(normed_out, cot_all[:, i * in_rows : (i + 1) * in_rows], ((0,), (0,)))

    grad_out_proj = scatter_dp(grad_out_part)

    def grad_in_part(cotangent):
        def part(i):
            return mm(normed_all[:, i * in_rows : (i + 1) * in_rows], cotangent, ((0,), (0,)))

        return part

    grad_in_gate = to_store(scatter_dp(grad_in_part(gate_grad)), gate_range)

    mixed_low = mixed_grad.astype(BF16).reshape(blocks, SPAN, heads, P_SIZE)
    mixed_back = mixed_low.astype(F32)
    grad_d_skip = jnp.sum(mixed_back * values_f, axis=(0, 1, 3))
    values_grad = skip_own[:, None] * mixed_back
    outer_low = (mixed_back * growth).astype(BF16)
    log_grad = jnp.sum(mixed_back * outer_out, axis=3)
    start_grads = jnp.einsum("kqn,kqhp->khpn", readout, outer_low, preferred_element_type=F32)
    readout_grad = jnp.einsum("kqhp,khpn->kqn", outer_low, starts_low, preferred_element_type=F32)
    mix_grad = jnp.einsum("kqhp,kshp->khqs", mixed_low, values_b, preferred_element_type=F32)
    values_grad = values_grad + jnp.einsum(
        "khqs,kqhp->kshp", mix_weights, mixed_low, preferred_element_type=F32
    )
    through = mix_grad * mix_full
    log_grad = (
        log_grad
        + jnp.transpose(jnp.sum(through, axis=3), (0, 2, 1))
        - jnp.transpose(jnp.sum(through, axis=2), (0, 2, 1))
    )
    decayed_grad = mix_grad * decay_table
    score_grad = jnp.sum(decayed_grad * step_by_head[:, :, None, :], axis=1).astype(BF16)
    step_grad = jnp.transpose(jnp.sum(decayed_grad * scores[:, None], axis=2), (0, 2, 1))
    readout_grad = readout_grad + jnp.einsum(
        "kqs,ksn->kqn", score_grad, inputs_b, preferred_element_type=F32
    )
    inputs_grad = jnp.einsum("kqs,kqn->ksn", score_grad, readout, preferred_element_type=F32)
    carried = jnp.zeros((heads, P_SIZE, N), F32)
    state_grads = [None] * blocks
    for k in range(blocks - 1, -1, -1):
        state_grads[k] = carried
        carried = start_grads[k] + total_exp[k][:, None, None] * carried
    state_grads = jnp.stack(state_grads)
    total_grad = total_exp * jnp.sum(state_grads * starts, axis=(2, 3))
    state_low = state_grads.astype(BF16)
    weighted_grad = jnp.einsum("khpn,ksn->kshp", state_low, inputs_b, preferred_element_type=F32)
    inputs_grad = inputs_grad + jnp.einsum(
        "kshp,khpn->ksn", weighted, state_low, preferred_element_type=F32
    )
    values_grad = values_grad + weighted_grad * tail_weight[..., None]
    tail_grad = jnp.sum(weighted_grad * values_f, axis=3)
    tail_term = tail_grad * tail_weight
    step_grad = step_grad + tail_grad * tail_exp
    log_grad = log_grad - tail_term
    log_grad = log_grad.at[:, -1, :].add(jnp.sum(tail_term, axis=1) + total_grad)
    decay_grad = jnp.flip(jnp.cumsum(jnp.flip(log_grad, 1), axis=1), 1)
    step_grad = step_grad + decay_grad * decay_rate
    grad_a_log = jnp.sum(decay_grad * step_size, axis=(0, 1)) * decay_rate
    raw_grad = step_grad.reshape(seq_rows, heads) * jax.nn.sigmoid(pre_act)
    grad_dt_bias = jnp.sum(raw_grad, axis=0)

    act_grad = jnp.concatenate(
        [
            values_grad.reshape(seq_rows, cols),
            inputs_grad.reshape(seq_rows, N),
            readout_grad.reshape(seq_rows, N),
        ],
        axis=1,
    )
    conv_sig = jax.nn.sigmoid(convolved)
    conv_grad = act_grad * (conv_sig * (1.0 + convolved * (1.0 - conv_sig)))
    bias_cols = jnp.sum(conv_grad, axis=0)
    taps_cols = jnp.stack(
        [jnp.sum(conv_grad * padded[offset : offset + seq_rows], axis=0) for offset in range(CONV)]
    )
    after = jnp.pad(conv_grad, ((0, CONV - 1), (0, 0)))
    inner_grad = taps[CONV - 1] * conv_grad
    for offset in range(CONV - 1):
        back = CONV - 1 - offset
        inner_grad = inner_grad + taps[offset] * after[back : back + seq_rows]
    raw_wide = lax.dynamic_update_slice_in_dim(
        jnp.zeros((seq_rows, H), F32), raw_grad, own_heads, 1
    )
    x_grad = jnp.concatenate([inner_grad.astype(BF16), raw_wide.astype(BF16)], axis=1)

    grad_in_x = scatter_dp(grad_in_part(x_grad))
    grad_in_proj = (
        grad_in_gate + to_store(grad_in_x[:, :cols], value_range) + to_store(grad_in_x[:, cols:], tail_range)
    )

    gate_rows = gate_grad.reshape(groups, tok_rows, cols)
    x_rows = x_grad.reshape(groups, tok_rows, cols + tail)

    def normed_part(i):
        return mm(lax.dynamic_index_in_dim(gate_rows, i, 0, keepdims=False), w_g, ((1,), (1,))) + mm(
            lax.dynamic_index_in_dim(x_rows, i, 0, keepdims=False), w_x, ((1,), (1,))
        )

    normed_grad = reorder(scatter_state(normed_part), "dp")
    pushed = normed_grad * norm_in_gain
    token_grad = in_scale * pushed - tokens * (
        in_scale * in_scale * in_scale * jnp.mean(pushed * tokens, axis=-1, keepdims=True)
    )
    grad_input = out_cotangent.astype(F32) + token_grad
    grad_norm_in = jnp.sum(normed_grad * tokens * in_scale, axis=0)

    def spread(entries, total, at):
        return lax.dynamic_update_slice_in_dim(
            jnp.zeros(entries.shape[:-1] + (total,), F32), entries, at, entries.ndim - 1
        )

    taps_wide = spread(taps_cols[:, :cols], xbc, cols * group).at[:, inner:].set(taps_cols[:, cols:])
    bias_wide = spread(bias_cols[:cols], xbc, cols * group).at[inner:].set(bias_cols[cols:])
    flat = [
        taps_wide.reshape(-1),
        bias_wide,
        spread(grad_dt_bias, H, own_heads),
        spread(grad_a_log, H, own_heads),
        spread(grad_d_skip, H, own_heads),
        grad_norm_in,
        spread(grad_norm_out, inner, cols * group),
    ]
    sizes = [entry.shape[0] for entry in flat]
    packed = jnp.concatenate(flat)
    packed = jnp.pad(packed, (0, -packed.shape[0] % 1024)).reshape(-1, 128)
    packed = sum_axis(sum_axis(packed, "dp"), "state").reshape(-1)
    summed = []
    at = 0
    for size in sizes:
        summed.append(packed[at : at + size])
        at += size
    return (
        block_out,
        grad_input,
        grad_in_proj,
        grad_out_proj,
        summed[0].reshape(CONV, xbc),
        summed[1],
        summed[2],
        summed[3],
        summed[4],
        summed[5],
        summed[6],
    )


def solution(mesh):
    rows = P(("dp", "state"), None)
    whole = P()
    in_specs = (rows, P("dp"), P("dp", "state"), P("state", "dp")) + (whole,) * 7 + (rows,)
    out_specs = (rows, rows, P("dp", "state"), P("state", "dp")) + (whole,) * 7
    return jax.shard_map(local, mesh=mesh, in_specs=in_specs, out_specs=out_specs, check_vma=False)
```

```python
import jax
import jax.numpy as jnp
from jax import lax
from jax.experimental import pallas as pl
from jax.experimental.pallas import tpu as pltpu
from jax.sharding import PartitionSpec as P

H = 64
P_SIZE = 64
N = 128
SPAN = 256
CONV = 4
EPSILON = 1e-05
F32 = jnp.float32
BF16 = jnp.bfloat16


def mm(left, right, dims):
    return lax.dot_general(left, right, (dims, ((), ())), preferred_element_type=F32)


def flip(value, axis, bit):
    count = lax.axis_size(axis)
    return lax.ppermute(value, axis, [(i, i ^ bit) for i in range(count)])


def window(piece, piece_start, start, width):
    have = piece.shape[1]
    padded = jnp.pad(piece, ((0, 0), (width, width)))
    offset = jnp.clip(start - piece_start + width, 0, have + width)
    return lax.dynamic_slice_in_dim(padded, offset, width, 1)


def moves(count, from_range, to_range):
    found = {}
    for source in range(count):
        for target in range(count):
            a, b = from_range(source), to_range(target)
            if source != target and max(a[0], b[0]) < min(a[1], b[1]):
                found.setdefault(target - source, []).append((source, target))
    return found


def gather_state(own):
    count, here = lax.axis_size("state"), lax.axis_index("state")
    out = jnp.zeros((count,) + own.shape, own.dtype)
    held = {0: own}
    bit = count // 2
    while bit:
        for key in list(held):
            held[key | bit] = flip(held[key], "state", bit)
        bit //= 2
    for key, part in held.items():
        out = lax.dynamic_update_index_in_dim(out, part, here ^ key, 0)
    return out


def slots(axis):
    count = lax.axis_size(axis)
    return [(step, other) for step in range(count // 2) for other in range(2)]


def ringed(axis):
    return lax.axis_size(axis) <= 8


def reorder(value, axis):
    if not ringed(axis):
        return value
    count, here = lax.axis_size(axis), lax.axis_index(axis)
    steps = count // 2
    rows, width = value.shape
    pieces = [value[:, i * (width // steps) : (i + 1) * (width // steps)] for i in range(steps)][::-1]
    pair = width // count
    turned = jnp.concatenate(pieces + pieces[:-1], axis=1)
    turned = lax.dynamic_slice_in_dim(turned, (steps - 1 - here // 2) * 2 * pair, width, 1)
    halves = [turned[:, i * pair : (i + 1) * pair] for i in range(count)]
    swapped = jnp.concatenate([halves[i ^ 1] for i in range(count)], axis=1)
    return jnp.where(here % 2 == 0, turned, swapped)


def gather_dp(own):
    count = lax.axis_size("dp")
    if not ringed("dp"):
        every = lax.all_gather(own, "dp")
        return [every[i] for i in range(count)]
    ring = [(i, (i + 2) % count) for i in range(count)]
    out = []
    held = own
    for step in range(count // 2):
        out += [held, flip(held, "dp", 1)]
        if step + 1 < count // 2:
            held = lax.ppermute(held, "dp", ring)
    return out


def scatter_dp(part_of):
    count = lax.axis_size("dp")
    if not ringed("dp"):
        parts = jnp.stack([part_of(i) for i in range(count)])
        return lax.psum_scatter(parts, "dp", scatter_dimension=0, tiled=False)
    ring = [(i, (i + 2) % count) for i in range(count)]
    carried = None
    for step in range(1, count // 2 + 1):
        at = 2 * (step % (count // 2))
        total = part_of(at) + flip(part_of(at + 1).astype(BF16), "dp", 1).astype(F32)
        if carried is not None:
            total = total + carried.astype(F32)
        if step < count // 2:
            carried = lax.ppermute(total.astype(BF16), "dp", ring)
    return total


def scatter_state(part_of):
    count, here = lax.axis_size("state"), lax.axis_index("state")

    order = []
    bit = 1
    while bit < count:
        order.append(bit)
        bit *= 2
    parts = {key: part_of(here ^ key) for key in range(count)}
    for bit in order:
        for key in [k for k in parts if not k & bit]:
            sent = flip(parts.pop(key | bit).astype(BF16), "state", bit)
            parts[key] = parts[key] + sent.astype(F32)
    return parts[0]


def sum_axis(value, axis):
    bit = 1
    while bit < lax.axis_size(axis):
        value = value + flip(value, axis, bit)
        bit *= 2
    return value


def spans(size):
    half = size // 2
    return [(0, half, half), (half, size, size)]


def dots(left, right, contract, exact=False):
    return lax.dot_general(
        left,
        right,
        (contract, ((), ())),
        preferred_element_type=F32,
        precision=lax.Precision.HIGHEST if exact else None,
    )


def softplus(value):
    return jnp.maximum(value, 0.0) + jnp.log1p(jnp.exp(-jnp.abs(value)))


def triangle(size, upper):
    row = lax.broadcasted_iota(jnp.int32, (size, size), 0)
    col = lax.broadcasted_iota(jnp.int32, (size, size), 1)
    return (row <= col if upper else row >= col).astype(F32)


def decays(raw, place, bias, bias_t, rate, rate_t):
    pre = dots(raw, place, ((1,), (1,))) + bias
    pre_t = dots(place, raw, ((1,), (1,))) + bias_t
    step, step_t = softplus(pre), softplus(pre_t)
    size = raw.shape[0]
    log = dots(triangle(size, False), step * rate, ((1,), (0,)), True)
    log_t = dots(step_t * rate_t, triangle(size, True), ((1,), (0,)), True)
    return pre, step, step_t, log, log_t


def decay_of(log, log_t, head, span):
    first, last, seen = span
    gap = log[first:last, head : head + 1] - log_t[head : head + 1, :seen]
    row = first + lax.broadcasted_iota(jnp.int32, gap.shape, 0)
    col = lax.broadcasted_iota(jnp.int32, gap.shape, 1)
    return jnp.exp(jnp.where(row >= col, gap, -jnp.inf))


def convolve(before, here, taps, bias):
    ext = jnp.concatenate([before, here], axis=0)
    size = here.shape[0]
    start = before.shape[0] - (CONV - 1)
    total = bias + taps[0:1] * ext[start : start + size]
    for offset in range(1, CONV):
        total = total + taps[offset : offset + 1] * ext[start + offset : start + offset + size]
    return total, ext


def scan_forward(
    x_ref, taps_ref, cbias_ref, place_ref, bias_ref, bias_t_ref, rate_ref, rate_t_ref, skip_ref,
    act_ref, mixed_ref, starts_ref, halo, state,
):
    @pl.when(pl.program_id(0) == 0)
    def _():
        halo[...] = jnp.zeros_like(halo)
        state[...] = jnp.zeros_like(state)

    size = x_ref.shape[0]
    heads = place_ref.shape[0]
    cols = heads * P_SIZE
    wide = cols + 2 * N
    for at in range(0, wide, 128):
        here = x_ref[:, at : at + 128].astype(F32)
        conv, _ = convolve(halo[:, at : at + 128], here, taps_ref[:, at : at + 128], cbias_ref[:, at : at + 128])
        act_ref[:, at : at + 128] = (conv * jax.nn.sigmoid(conv)).astype(BF16)
        halo[:, at : at + 128] = here[size - 8 :]
    _, step, step_t, log, log_t = decays(
        x_ref[:, wide:], place_ref[...], bias_ref[...], bias_t_ref[...], rate_ref[...], rate_t_ref[...]
    )
    growth = jnp.exp(log)
    tail = jnp.exp(log[size - 1 :] - log) * step
    inputs_b = act_ref[:, cols : cols + N]
    readout = act_ref[:, cols + N :]
    scores = dots(readout, inputs_b, ((1,), (1,)))
    left = lax.broadcasted_iota(jnp.int32, (size, 128), 1) < P_SIZE
    upper = lax.broadcasted_iota(jnp.int32, (128, 128), 0) < P_SIZE
    for pair in range(heads // 2):
        at = pair * 128
        a, b = 2 * pair, 2 * pair + 1
        vals = act_ref[:, at : at + 128]
        vals_f = vals.astype(F32)
        held = state[at : at + 128, :]
        starts_ref[at : at + 128, :] = held
        outer = dots(readout, held.astype(BF16), ((1,), (1,)))
        base = jnp.where(left, growth[:, a : a + 1], growth[:, b : b + 1]) * outer + skip_ref[:, at : at + 128] * vals_f
        split = [jnp.where(left, vals, 0), jnp.where(left, 0, vals)]
        for span in spans(size):
            first, last, seen = span
            total = base[first:last]
            for head, part in ((a, split[0]), (b, split[1])):
                mix = scores[first:last, :seen] * decay_of(log, log_t, head, span) * step_t[head : head + 1, :seen]
                total = total + dots(mix.astype(BF16), part[:seen], ((1,), (0,)))
            mixed_ref[first:last, at : at + 128] = total
        low = (vals_f * jnp.where(left, tail[:, a : a + 1], tail[:, b : b + 1])).astype(BF16)
        keep = jnp.where(upper, growth[size - 1 :, a : a + 1], growth[size - 1 :, b : b + 1])
        state[at : at + 128, :] = keep * held + dots(low, inputs_b, ((0,), (0,)))


def scan_backward(
    x_ref, before_ref, act_ref, grad_ref, starts_ref,
    taps_ref, cbias_ref, place_ref, bias_ref, bias_t_ref, rate_ref, rate_t_ref, skip_ref,
    out_ref, conv_ref, skip_grad_ref, head_ref,
    after, state, by_col, by_row, tails, score_sum, in_grad, read_grad,
):
    turn = pl.program_id(0)

    @pl.when(turn == 0)
    def _():
        after[...] = jnp.zeros_like(after)
        state[...] = jnp.zeros_like(state)
        conv_ref[...] = jnp.zeros_like(conv_ref)
        skip_grad_ref[...] = jnp.zeros_like(skip_grad_ref)
        head_ref[...] = jnp.zeros_like(head_ref)

    is_first = turn == pl.num_programs(0) - 1
    size = x_ref.shape[0]
    heads = place_ref.shape[0]
    cols = heads * P_SIZE
    wide = cols + 2 * N
    place = place_ref[...]
    pre, step, step_t, log, log_t = decays(
        x_ref[:, wide:], place, bias_ref[...], bias_t_ref[...], rate_ref[...], rate_t_ref[...]
    )
    growth = jnp.exp(log)
    tail_exp = jnp.exp(log[size - 1 :] - log)
    tail = tail_exp * step
    inputs_b = act_ref[:, cols : cols + N]
    readout = act_ref[:, cols + N :]
    scores = dots(readout, inputs_b, ((1,), (1,)))
    left = lax.broadcasted_iota(jnp.int32, (size, 128), 1) < P_SIZE
    upper = lax.broadcasted_iota(jnp.int32, (128, 128), 0) < P_SIZE

    def through_conv(at, grad):
        here = x_ref[:, at : at + 128].astype(F32)
        before = jnp.where(is_first, 0.0, before_ref[8:, at : at + 128].astype(F32))
        taps = taps_ref[:, at : at + 128]
        conv, ext = convolve(before, here, taps, cbias_ref[:, at : at + 128])
        sig = jax.nn.sigmoid(conv)
        grad = grad * (sig * (1.0 + conv * (1.0 - sig)))
        start = 8 - (CONV - 1)
        rows = [jnp.sum(grad * ext[start + o : start + o + size], axis=0, keepdims=True) for o in range(CONV)]
        rows += [jnp.sum(grad, axis=0, keepdims=True), jnp.zeros((3, 128), F32)]
        conv_ref[:, at : at + 128] += jnp.concatenate(rows, axis=0)
        onward = jnp.concatenate([grad, after[:, at : at + 128]], axis=0)
        after[:, at : at + 128] = grad[:8]
        total = taps[CONV - 1 : CONV] * grad
        for o in range(CONV - 1):
            total = total + taps[o : o + 1] * onward[CONV - 1 - o : CONV - 1 - o + size]
        out_ref[:, at : at + 128] = total.astype(BF16)

    score_sum[...] = jnp.zeros_like(score_sum)
    in_grad[...] = jnp.zeros_like(in_grad)
    read_grad[...] = jnp.zeros_like(read_grad)
    for pair in range(heads // 2):
        at = pair * 128
        a, b = 2 * pair, 2 * pair + 1
        vals = act_ref[:, at : at + 128]
        vals_f = vals.astype(F32)
        grad = grad_ref[:, at : at + 128]
        grad_f = grad.astype(F32)
        starts = starts_ref[at : at + 128, :]
        starts_low = starts.astype(BF16)
        held = state[at : at + 128, :]
        held_low = held.astype(BF16)
        grown = grad_f * jnp.where(left, growth[:, a : a + 1], growth[:, b : b + 1])
        outer_low = grown.astype(BF16)
        outer = grown * dots(readout, starts_low, ((1,), (1,)))
        read_grad[...] += dots(outer_low, starts_low, ((1,), (0,)))
        tail_pair = jnp.where(left, tail[:, a : a + 1], tail[:, b : b + 1])
        low = (vals_f * tail_pair).astype(BF16)
        in_grad[...] += dots(low, held_low, ((1,), (0,)))
        low_grad = dots(inputs_b, held_low, ((1,), (1,)))
        tail_part = low_grad * vals_f
        product = grad_f * vals_f
        skip_grad_ref[:, at : at + 128] += jnp.sum(product, axis=0, keepdims=True)
        keep = jnp.where(upper, growth[size - 1 :, a : a + 1], growth[size - 1 :, b : b + 1])
        shared = jnp.sum(held * starts, axis=1, keepdims=True)
        state[at : at + 128, :] = dots(outer_low, readout, ((0,), (0,))) + keep * held
        base = skip_ref[:, at : at + 128] * grad_f + low_grad * tail_pair
        top = base[: size // 2]
        bottom = base[size // 2 :]
        for head, side in ((a, left), (b, jnp.logical_not(left))):
            own = jnp.where(side, grad, 0)
            tails[:, head : head + 1] = jnp.sum(jnp.where(side, tail_part, 0.0), axis=1, keepdims=True)
            rows = []
            sums = jnp.zeros((1, size), F32)
            for span in spans(size):
                first, last, seen = span
                mix_grad = dots(own[first:last], vals[:seen], ((1,), (1,)))
                decay = decay_of(log, log_t, head, span)
                steps = step_t[head : head + 1, :seen]
                some = scores[first:last, :seen]
                decayed = mix_grad * decay
                by_score = decayed * some
                score_sum[first:last, :seen] += decayed * steps
                rows.append(jnp.sum(by_score * steps, axis=1, keepdims=True))
                sums = sums + jnp.pad(jnp.sum(by_score, axis=0, keepdims=True), ((0, 0), (0, size - seen)))
                back = dots((some * decay * steps).astype(BF16), own[first:last], ((0,), (0,)))
                top = top + back[: size // 2]
                if seen == size:
                    bottom = bottom + back[size // 2 :]
            by_row[head : head + 1, :] = sums
            flow = jnp.sum(jnp.where(side, outer, 0.0), axis=1, keepdims=True)
            by_col[:, head : head + 1] = jnp.concatenate(rows, axis=0) + flow
            half = shared[:P_SIZE] if head == a else shared[P_SIZE:]
            by_col[size - 1 :, head : head + 1] += growth[size - 1 :, head : head + 1] * jnp.sum(
                half, axis=0, keepdims=True
            )
        through_conv(at, jnp.concatenate([top, bottom], axis=0))

    score_grad = score_sum[...].astype(BF16)
    through_conv(cols, in_grad[...] + dots(score_grad, readout, ((0,), (0,))))
    through_conv(cols + N, read_grad[...] + dots(score_grad, inputs_b, ((1,), (0,))))

    eye = (
        lax.broadcasted_iota(jnp.int32, (heads, heads), 0) == lax.broadcasted_iota(jnp.int32, (heads, heads), 1)
    ).astype(F32)
    summed = dots(by_row[...], eye, ((0,), (0,)), True)
    tail_grad = tails[...]
    tail_term = tail_grad * tail
    log_grad = by_col[...] - step * summed - tail_term
    row = lax.broadcasted_iota(jnp.int32, log_grad.shape, 0)
    log_grad = log_grad + jnp.where(row == size - 1, jnp.sum(tail_term, axis=0, keepdims=True), 0.0)
    decay_grad = dots(triangle(size, True), log_grad, ((1,), (0,)), True)
    step_grad = summed + tail_grad * tail_exp + decay_grad * rate_ref[...]
    raw = step_grad * jax.nn.sigmoid(pre)
    head_ref[...] += jnp.concatenate(
        [
            jnp.sum(raw, axis=0, keepdims=True),
            jnp.sum(decay_grad * step, axis=0, keepdims=True) * rate_ref[...],
            jnp.zeros((6, heads), F32),
        ],
        axis=0,
    )
    out_ref[:, wide:] = dots(raw.astype(BF16), place, ((1,), (0,))).astype(BF16)


def whole_spec(value):
    return pl.BlockSpec(value.shape, lambda k: (0,) * value.ndim)


def run_scan_forward(x_proj, params):
    rows, width = x_proj.shape
    wide = params[0].shape[1]
    cols = wide - 2 * N
    blocks = rows // SPAN
    return pl.pallas_call(
        scan_forward,
        grid=(blocks,),
        in_specs=[pl.BlockSpec((SPAN, width), lambda k: (k, 0))] + [whole_spec(p) for p in params],
        out_specs=[
            pl.BlockSpec((SPAN, wide), lambda k: (k, 0)),
            pl.BlockSpec((SPAN, cols), lambda k: (k, 0)),
            pl.BlockSpec((cols, N), lambda k: (k, 0)),
        ],
        out_shape=[
            jax.ShapeDtypeStruct((rows, wide), BF16),
            jax.ShapeDtypeStruct((rows, cols), F32),
            jax.ShapeDtypeStruct((blocks * cols, N), F32),
        ],
        scratch_shapes=[pltpu.VMEM((8, wide), F32), pltpu.VMEM((cols, N), F32)],
        compiler_params=pltpu.CompilerParams(dimension_semantics=("arbitrary",)),
        name="scan_forward",
    )(x_proj, *params)


def run_scan_backward(x_proj, act, mixed_low, starts, params):
    rows, width = x_proj.shape
    wide = act.shape[1]
    cols = wide - 2 * N
    heads = cols // P_SIZE
    blocks = rows // SPAN
    last = blocks - 1
    return pl.pallas_call(
        scan_backward,
        grid=(blocks,),
        in_specs=[
            pl.BlockSpec((SPAN, width), lambda k: (last - k, 0)),
            pl.BlockSpec((16, width), lambda k: (jnp.maximum((last - k) * (SPAN // 16) - 1, 0), 0)),
            pl.BlockSpec((SPAN, wide), lambda k: (last - k, 0)),
            pl.BlockSpec((SPAN, cols), lambda k: (last - k, 0)),
            pl.BlockSpec((cols, N), lambda k: (last - k, 0)),
        ]
        + [whole_spec(p) for p in params],
        out_specs=[
            pl.BlockSpec((SPAN, width), lambda k: (last - k, 0)),
            pl.BlockSpec((8, wide), lambda k: (0, 0)),
            pl.BlockSpec((1, cols), lambda k: (0, 0)),
            pl.BlockSpec((8, heads), lambda k: (0, 0)),
        ],
        out_shape=[
            jax.ShapeDtypeStruct((rows, width), BF16),
            jax.ShapeDtypeStruct((8, wide), F32),
            jax.ShapeDtypeStruct((1, cols), F32),
            jax.ShapeDtypeStruct((8, heads), F32),
        ],
        scratch_shapes=[
            pltpu.VMEM((8, wide), F32),
            pltpu.VMEM((cols, N), F32),
            pltpu.VMEM((SPAN, heads), F32),
            pltpu.VMEM((heads, SPAN), F32),
            pltpu.VMEM((SPAN, heads), F32),
            pltpu.VMEM((SPAN, SPAN), F32),
            pltpu.VMEM((SPAN, N), F32),
            pltpu.VMEM((SPAN, N), F32),
        ],
        compiler_params=pltpu.CompilerParams(dimension_semantics=("arbitrary",)),
        name="scan_backward",
    )(x_proj, x_proj, act, mixed_low, starts, *params)


def local(
    block_input,
    width_index,
    w_in,
    w_out,
    conv_weight,
    conv_bias,
    dt_bias,
    a_log,
    d_skip,
    norm_in_gain,
    norm_out_gain,
    out_cotangent,
):
    tok_rows, width = block_input.shape
    inner = H * P_SIZE
    xbc = inner + 2 * N
    full_cols = 2 * inner + 2 * N + H
    groups, group = lax.axis_size("state"), lax.axis_index("state")
    seq_rows = tok_rows * groups
    heads = H // groups
    cols = inner // groups
    store = full_cols // groups
    in_rows = w_in.shape[0]
    tail = 2 * N + H

    def store_range(i):
        return (store * i, store * (i + 1))

    def value_range(i):
        return (inner + cols * i, inner + cols * (i + 1))

    def gate_range(i):
        return (cols * i, cols * (i + 1))

    def tail_range(i):
        return (inner + inner, full_cols)

    def from_store(wanted):
        size = wanted(0)[1] - wanted(0)[0]
        total = window(w_in, store * group, wanted(group)[0], size)
        for shift, pairs in moves(groups, store_range, wanted).items():
            sent = window(w_in, store * group, wanted(group + shift)[0], size)
            total = total + lax.ppermute(sent, "state", pairs)
        return total

    def to_store(piece, held):
        piece = piece.astype(BF16)
        total = window(piece, held(group)[0], store * group, store).astype(F32)
        for shift, pairs in moves(groups, held, store_range).items():
            came = lax.ppermute(piece, "state", pairs)
            total = total + window(came, held(group - shift)[0], store * group, store).astype(F32)
        return total

    tokens = block_input.astype(F32)
    in_scale = lax.rsqrt(jnp.mean(tokens * tokens, axis=-1, keepdims=True) + EPSILON)
    normed = (tokens * in_scale * norm_in_gain).astype(BF16)

    w_x_own = jnp.concatenate([from_store(value_range), from_store(tail_range)], axis=1)
    w_x = jnp.concatenate(gather_dp(w_x_own), axis=0)
    normed_all = gather_state(reorder(normed, "dp")).reshape(seq_rows, width)
    w_g = jnp.concatenate(gather_dp(from_store(gate_range)), axis=0)
    w_o = jnp.concatenate(gather_dp(w_out), axis=1)
    cot_all = gather_state(reorder(out_cotangent, "dp")).reshape(seq_rows, width)

    x_proj = mm(normed_all, w_x, ((1,), (0,))).astype(BF16)
    own_heads = heads * group

    def own(entries, at, size):
        return lax.dynamic_slice_in_dim(entries, at, size, entries.ndim - 1)

    taps = jnp.concatenate([own(conv_weight, cols * group, cols), conv_weight[:, inner:]], axis=1)
    bias = jnp.concatenate([own(conv_bias, cols * group, cols), conv_bias[inner:]], axis=0)[None]
    gain_own = own(norm_out_gain, cols * group, cols)
    dt_own = own(dt_bias, own_heads, heads)
    rate_own = -jnp.exp(own(a_log, own_heads, heads))
    skip_own = jnp.repeat(own(d_skip, own_heads, heads), P_SIZE)[None]
    place = (own_heads + jnp.arange(heads)[:, None] == jnp.arange(H)[None, :]).astype(BF16)
    scan_params = (taps, bias, place, dt_own[None], dt_own[:, None], rate_own[None], rate_own[:, None], skip_own)
    act, mixed, starts = run_scan_forward(x_proj, scan_params)

    gate_part = mm(normed_all, w_g, ((1,), (0,))).astype(BF16).astype(F32)
    out_grad = mm(cot_all, w_o, ((1,), (1,)))
    heads_on = H // 8 * jnp.left_shift(1, width_index[0])
    mask = ((cols * group + jnp.arange(cols)) // P_SIZE < heads_on).astype(F32)
    active = (heads_on * P_SIZE).astype(F32)
    gate_sig = jax.nn.sigmoid(gate_part)
    gate_act = gate_part * gate_sig
    gated = mixed * gate_act
    weighted_grad_out = out_grad * (gain_own * mask)
    stats = jnp.stack(
        [jnp.sum(mask * gated * gated, axis=-1), jnp.sum(weighted_grad_out * gated, axis=-1)]
    )
    stats = lax.psum(stats, "state")
    out_scale = lax.rsqrt(stats[0] / active + EPSILON)[:, None]
    pull = (stats[1] / active)[:, None] * out_scale * out_scale * out_scale
    normed_out = (gated * out_scale * (gain_own * mask)).astype(BF16)
    grad_norm_out = jnp.sum(out_grad * mask * gated * out_scale, axis=0)
    gated_grad = weighted_grad_out * out_scale - gated * mask * pull
    mixed_grad = gated_grad * gate_act
    gate_grad = (gated_grad * mixed * (gate_sig * (1.0 + gate_part * (1.0 - gate_sig)))).astype(BF16)

    rows_of = normed_out.reshape(groups, tok_rows, cols)

    def out_part(i):
        rows = lax.dynamic_index_in_dim(rows_of, i, 0, keepdims=False)
        return mm(rows, w_o, ((1,), (0,)))

    block_out = (tokens + reorder(scatter_state(out_part), "dp")).astype(BF16)

    def grad_out_part(i):
        return mm(normed_out, cot_all[:, i * in_rows : (i + 1) * in_rows], ((0,), (0,)))

    grad_out_proj = scatter_dp(grad_out_part)

    def grad_in_part(cotangent):
        def part(i):
            return mm(normed_all[:, i * in_rows : (i + 1) * in_rows], cotangent, ((0,), (0,)))

        return part

    grad_in_gate = to_store(scatter_dp(grad_in_part(gate_grad)), gate_range)

    x_grad, conv_sums, skip_sums, head_sums = run_scan_backward(
        x_proj, act, mixed_grad.astype(BF16), starts, scan_params
    )
    taps_cols, bias_cols = conv_sums[:CONV], conv_sums[CONV]
    grad_d_skip = jnp.sum(skip_sums.reshape(heads, P_SIZE), axis=1)
    grad_dt_bias, grad_a_log = head_sums[0], head_sums[1]

    grad_in_x = scatter_dp(grad_in_part(x_grad))
    grad_in_proj = (
        grad_in_gate + to_store(grad_in_x[:, :cols], value_range) + to_store(grad_in_x[:, cols:], tail_range)
    )

    gate_rows = gate_grad.reshape(groups, tok_rows, cols)
    x_rows = x_grad.reshape(groups, tok_rows, cols + tail)

    def normed_part(i):
        return mm(lax.dynamic_index_in_dim(gate_rows, i, 0, keepdims=False), w_g, ((1,), (1,))) + mm(
            lax.dynamic_index_in_dim(x_rows, i, 0, keepdims=False), w_x, ((1,), (1,))
        )

    normed_grad = reorder(scatter_state(normed_part), "dp")
    pushed = normed_grad * norm_in_gain
    token_grad = in_scale * pushed - tokens * (
        in_scale * in_scale * in_scale * jnp.mean(pushed * tokens, axis=-1, keepdims=True)
    )
    grad_input = out_cotangent.astype(F32) + token_grad
    grad_norm_in = jnp.sum(normed_grad * tokens * in_scale, axis=0)

    def spread(entries, total, at):
        return lax.dynamic_update_slice_in_dim(
            jnp.zeros(entries.shape[:-1] + (total,), F32), entries, at, entries.ndim - 1
        )

    taps_wide = spread(taps_cols[:, :cols], xbc, cols * group).at[:, inner:].set(taps_cols[:, cols:])
    bias_wide = spread(bias_cols[:cols], xbc, cols * group).at[inner:].set(bias_cols[cols:])
    flat = [
        taps_wide.reshape(-1),
        bias_wide,
        spread(grad_dt_bias, H, own_heads),
        spread(grad_a_log, H, own_heads),
        spread(grad_d_skip, H, own_heads),
        grad_norm_in,
        spread(grad_norm_out, inner, cols * group),
    ]
    sizes = [entry.shape[0] for entry in flat]
    packed = jnp.concatenate(flat)
    packed = jnp.pad(packed, (0, -packed.shape[0] % 1024)).reshape(-1, 128)
    packed = sum_axis(sum_axis(packed, "dp"), "state").reshape(-1)
    summed = []
    at = 0
    for size in sizes:
        summed.append(packed[at : at + size])
        at += size
    return (
        block_out,
        grad_input,
        grad_in_proj,
        grad_out_proj,
        summed[0].reshape(CONV, xbc),
        summed[1],
        summed[2],
        summed[3],
        summed[4],
        summed[5],
        summed[6],
    )


def solution(mesh):
    rows = P(("dp", "state"), None)
    whole = P()
    in_specs = (rows, P("dp"), P("dp", "state"), P("state", "dp")) + (whole,) * 7 + (rows,)
    out_specs = (rows, rows, P("dp", "state"), P("state", "dp")) + (whole,) * 7
    return jax.shard_map(local, mesh=mesh, in_specs=in_specs, out_specs=out_specs, check_vma=False)
```

```python
import functools

import jax
import jax.numpy as jnp
from jax import lax
from jax.experimental import pallas as pl
from jax.experimental.pallas import tpu as pltpu
from jax.sharding import PartitionSpec as P

H = 64
P_SIZE = 64
N = 128
SPAN = 256
CONV = 4
EPSILON = 1e-05
F32 = jnp.float32
BF16 = jnp.bfloat16


def flip(value, axis, bit):
    return lax.ppermute(value, axis, [(i, i ^ bit) for i in range(lax.axis_size(axis))])


def moves(count, from_range, to_range):
    found = {}
    for source in range(count):
        for target in range(count):
            a, b = from_range(source), to_range(target)
            if source != target and max(a[0], b[0]) < min(a[1], b[1]):
                found.setdefault(target - source, []).append((source, target))
    return found


def stack_rows(parts, places):
    rows, width = parts[0].shape

    def kernel(places_ref, *refs):
        out = refs[-1]
        for i, part in enumerate(refs[:-1]):
            out[pl.ds(pl.multiple_of(places_ref[i] * rows, rows), rows), :] = part[...]

    return pl.pallas_call(
        kernel,
        in_specs=[pl.BlockSpec(memory_space=pltpu.SMEM)]
        + [pl.BlockSpec(memory_space=pltpu.VMEM) for _ in parts],
        out_specs=pl.BlockSpec(memory_space=pltpu.VMEM),
        out_shape=jax.ShapeDtypeStruct((rows * len(parts), width), parts[0].dtype),
    )(places, *parts)


def gather_state(own):
    count, here = lax.axis_size("state"), lax.axis_index("state")
    held = {0: own}
    bit = count // 2
    while bit:
        for key in list(held):
            held[key | bit] = flip(held[key], "state", bit)
        bit //= 2
    keys = sorted(held)
    return stack_rows([held[key] for key in keys], here ^ jnp.array(keys))


def ringed(axis):
    return lax.axis_size(axis) <= 8


def to_ring(value, axis):
    if not ringed(axis):
        return value
    count, here = lax.axis_size(axis), lax.axis_index(axis)
    steps = count // 2
    pair = value.shape[1] // count
    sides = []
    for side in range(2):
        blocks = [value[:, (2 * i + side) * pair : (2 * i + side + 1) * pair] for i in range(steps)][::-1]
        turned = jnp.concatenate(blocks + blocks[:-1], axis=1)
        sides.append(lax.dynamic_slice_in_dim(turned, (steps - 1 - here // 2) * pair, steps * pair, 1))
    even = here % 2 == 0
    return jnp.concatenate([jnp.where(even, *sides), jnp.where(even, *sides[::-1])], axis=1)


def from_ring(value, axis):
    if not ringed(axis):
        return value
    count, here = lax.axis_size(axis), lax.axis_index(axis)
    steps = count // 2
    pair = value.shape[1] // count
    first, second = value[:, : steps * pair], value[:, steps * pair :]
    even = here % 2 == 0
    sides = []
    for side in (jnp.where(even, first, second), jnp.where(even, second, first)):
        blocks = [side[:, i * pair : (i + 1) * pair] for i in range(steps)][::-1]
        turned = jnp.concatenate(blocks + blocks[:-1], axis=1)
        sides.append(lax.dynamic_slice_in_dim(turned, (steps - 1 - here // 2) * pair, steps * pair, 1))
    return jnp.concatenate(
        [sides[i % 2][:, i // 2 * pair : (i // 2 + 1) * pair] for i in range(count)], axis=1
    )


def gather_dp(own):
    count = lax.axis_size("dp")
    if not ringed("dp"):
        return [lax.all_gather(own, "dp", axis=1, tiled=True)]
    ring = [(i, (i + 2) % count) for i in range(count)]
    mine, other = [own], []
    for step in range(count // 2):
        other.append(flip(mine[step], "dp", 1))
        if step + 1 < count // 2:
            mine.append(lax.ppermute(mine[step], "dp", ring))
    return mine + other


def scatter_dp(left, right):
    count = lax.axis_size("dp")

    def multiply(some, kind):
        return lax.dot_general(left, some, (((0,), (0,)), ((), ())), preferred_element_type=kind)

    if not ringed("dp"):
        return lax.psum_scatter(multiply(right, F32), "dp", scatter_dimension=1, tiled=True)
    steps = count // 2
    half = right.shape[1] // 2
    wide = half // steps
    ring = [(i, (i + 2) % count) for i in range(count)]
    other = multiply(right[:, half:], BF16)
    mine = multiply(right[:, :half], BF16)
    carried = None
    for step in range(1, steps + 1):
        at = step % steps * wide
        came = flip(other[:, at : at + wide], "dp", 1)
        total = mine[:, at : at + wide].astype(F32) + came.astype(F32)
        if carried is not None:
            total = total + carried.astype(F32)
        if step < steps:
            carried = lax.ppermute(total.astype(BF16), "dp", ring)
    return total


def scatter_state(whole):
    count, here = lax.axis_size("state"), lax.axis_index("state")
    rows = whole.reshape(count, whole.shape[0] // count, whole.shape[1])
    parts = {key: lax.dynamic_index_in_dim(rows, here ^ key, 0, keepdims=False) for key in range(count)}
    bit = 1
    while bit < count:
        for key in [k for k in parts if not k & bit]:
            sent = flip(parts.pop(key | bit).astype(BF16), "state", bit)
            parts[key] = parts[key].astype(F32) + sent.astype(F32)
        bit *= 2
    return parts[0]


def sum_axis(value, axis):
    bits = []
    while 1 << len(bits) < lax.axis_size(axis):
        bits.append(1 << len(bits))
    for bit in bits:
        value = value + flip(value, axis, bit)
    return value


def meet(first, second):
    low, high = max(first[0], second[0]), min(first[1], second[1])
    return (low, high) if low < high else None


def cut_rows(own, group, plans):
    groups = len(plans[0])
    store, width = own.shape
    sizes = [max(sum(b - a for a, b in ranges) for ranges in plan if ranges) for plan in plans]

    def kernel(group_ref, own_ref, *outs):
        for out in outs:
            out[...] = jnp.zeros_like(out)
        for g in range(groups):

            @pl.when(group_ref[0] == g)
            def _():
                for out, plan in zip(outs, plans):
                    at = 0
                    for ask in plan[g] or []:
                        found = meet(ask, (store * g, store * (g + 1)))
                        if found:
                            low, high = found
                            out[at + low - ask[0] : at + high - ask[0], :] = own_ref[low - store * g : high - store * g, :]
                        at += ask[1] - ask[0]

    return pl.pallas_call(
        kernel,
        in_specs=[pl.BlockSpec(memory_space=pltpu.SMEM), pl.BlockSpec(memory_space=pltpu.VMEM)],
        out_specs=[pl.BlockSpec(memory_space=pltpu.VMEM) for _ in plans],
        out_shape=[jax.ShapeDtypeStruct((size, width), BF16) for size in sizes],
        name="cut_rows",
    )(group[None], own)


def paste_rows(pieces, group, plans, store):
    groups = len(plans[0])
    width = pieces[0].shape[1]

    def kernel(group_ref, *refs):
        out = refs[-1]
        out[...] = jnp.zeros_like(out)
        for g in range(groups):

            @pl.when(group_ref[0] == g)
            def _():
                for piece, plan in zip(refs[:-1], plans):
                    at = 0
                    for ask in plan[g] or []:
                        found = meet(ask, (store * g, store * (g + 1)))
                        if found:
                            low, high = found
                            out[low - store * g : high - store * g, :] += piece[
                                at + low - ask[0] : at + high - ask[0], :
                            ].astype(F32)
                        at += ask[1] - ask[0]

    return pl.pallas_call(
        kernel,
        in_specs=[pl.BlockSpec(memory_space=pltpu.SMEM)]
        + [pl.BlockSpec(memory_space=pltpu.VMEM) for _ in pieces],
        out_specs=pl.BlockSpec(memory_space=pltpu.VMEM),
        out_shape=jax.ShapeDtypeStruct((store, width), F32),
        name="paste_rows",
    )(group[None], *pieces)


def spans(size):
    half = size // 2
    return [(0, half, half), (half, size, size)]


def dots(left, right, contract, exact=False):
    return lax.dot_general(
        left,
        right,
        (contract, ((), ())),
        preferred_element_type=F32,
        precision=lax.Precision.HIGHEST if exact else None,
    )


def softplus(value):
    return jnp.maximum(value, 0.0) + jnp.log1p(jnp.exp(-jnp.abs(value)))


def triangle(size, upper):
    row = lax.broadcasted_iota(jnp.int32, (size, size), 0)
    col = lax.broadcasted_iota(jnp.int32, (size, size), 1)
    return (row <= col if upper else row >= col).astype(F32)


def decays(raw, place, bias, bias_t, rate, rate_t):
    pre = dots(raw, place, ((1,), (1,))) + bias
    pre_t = dots(place, raw, ((1,), (1,))) + bias_t
    step, step_t = softplus(pre), softplus(pre_t)
    size = raw.shape[0]
    log = dots(triangle(size, False), step * rate, ((1,), (0,)), True)
    log_t = dots(step_t * rate_t, triangle(size, True), ((1,), (0,)), True)
    return pre, step, step_t, log, log_t


def decay_of(log, log_t, head, span):
    first, last, seen = span
    gap = log[first:last, head : head + 1] - log_t[head : head + 1, :seen]
    row = first + lax.broadcasted_iota(jnp.int32, gap.shape, 0)
    col = lax.broadcasted_iota(jnp.int32, gap.shape, 1)
    return jnp.exp(jnp.where(row >= col, gap, -jnp.inf))


def convolve(before, here, taps, bias):
    ext = jnp.concatenate([before, here], axis=0)
    size = here.shape[0]
    start = before.shape[0] - (CONV - 1)
    total = bias + taps[0:1] * ext[start : start + size]
    for offset in range(1, CONV):
        total = total + taps[offset : offset + 1] * ext[start + offset : start + offset + size]
    return total, ext


def join(pieces, whole):
    @pl.when(pl.program_id(0) == 0)
    def _():
        wide = pieces[0].shape[1]
        for i, piece in enumerate(pieces):
            whole[:, i * wide : (i + 1) * wide] = piece[...]


def joined(pieces):
    return pltpu.VMEM((pieces[0].shape[0], sum(p.shape[1] for p in pieces)), BF16)


def row_of_sums(value):
    total = value[:, :128]
    for at in range(128, value.shape[1], 128):
        total = total + value[:, at : at + 128]
    return dots(jnp.ones((8, 128), F32), total, ((1,), (1,)), True)


def scan_forward(is_first, *refs):
    x_ref, taps_ref, cbias_ref, place_ref, bias_ref, bias_t_ref, rate_ref, rate_t_ref, skip_ref = refs[:9]
    act_ref, mixed_ref, starts_ref, halo, state = refs[-5:]

    @pl.when(pl.program_id(0) == 0)
    def _():
        for new, old in zip((halo, state), refs[-7:-5]):
            new[...] = jnp.zeros_like(new) if is_first else old[...]

    size = x_ref.shape[0]
    heads = place_ref.shape[0]
    cols = heads * P_SIZE
    wide = cols + 2 * N
    for at in range(0, wide, 128):
        here = x_ref[:, at : at + 128].astype(F32)
        conv, _ = convolve(halo[:, at : at + 128], here, taps_ref[:, at : at + 128], cbias_ref[:, at : at + 128])
        act_ref[:, at : at + 128] = (conv * jax.nn.sigmoid(conv)).astype(BF16)
        halo[:, at : at + 128] = here[size - 8 :]
    _, step, step_t, log, log_t = decays(
        x_ref[:, wide:], place_ref[...], bias_ref[...], bias_t_ref[...], rate_ref[...], rate_t_ref[...]
    )
    growth = jnp.exp(log)
    tail = jnp.exp(log[size - 1 :] - log) * step
    inputs_b = act_ref[:, cols : cols + N]
    readout = act_ref[:, cols + N :]
    scores = dots(readout, inputs_b, ((1,), (1,)))
    left = lax.broadcasted_iota(jnp.int32, (size, 128), 1) < P_SIZE
    upper = lax.broadcasted_iota(jnp.int32, (128, 128), 0) < P_SIZE
    for pair in range(heads // 2):
        at = pair * 128
        a, b = 2 * pair, 2 * pair + 1
        vals = act_ref[:, at : at + 128]
        vals_f = vals.astype(F32)
        held = state[at : at + 128, :]
        starts_ref[at : at + 128, :] = held
        outer = dots(readout, held.astype(BF16), ((1,), (1,)))
        base = jnp.where(left, growth[:, a : a + 1], growth[:, b : b + 1]) * outer + skip_ref[:, at : at + 128] * vals_f
        split = [jnp.where(left, vals, 0), jnp.where(left, 0, vals)]
        for span in spans(size):
            first, last, seen = span
            total = base[first:last]
            for head, part in ((a, split[0]), (b, split[1])):
                mix = scores[first:last, :seen] * decay_of(log, log_t, head, span) * step_t[head : head + 1, :seen]
                total = total + dots(mix.astype(BF16), part[:seen], ((1,), (0,)))
            mixed_ref[first:last, at : at + 128] = total
        low = (vals_f * jnp.where(left, tail[:, a : a + 1], tail[:, b : b + 1])).astype(BF16)
        keep = jnp.where(upper, growth[size - 1 :, a : a + 1], growth[size - 1 :, b : b + 1])
        state[at : at + 128, :] = keep * held + dots(low, inputs_b, ((0,), (0,)))


def scan_backward(is_last, is_first, *refs):
    (
        x_ref, before_ref, act_ref, grad_ref, starts_ref,
        taps_ref, cbias_ref, place_ref, bias_ref, bias_t_ref, rate_ref, rate_t_ref, skip_ref,
    ) = refs[:13]
    olds = refs[13:-12]
    out_ref, *news = refs[-12:-6]
    by_col, by_row, tails, score_sum, in_grad, read_grad = refs[-6:]
    for i, new in enumerate(news):
        new[...] = jnp.zeros_like(new) if is_last else olds[i + 1][...]
    after, state, conv_ref, skip_grad_ref, head_ref = news
    size = x_ref.shape[0]
    heads = place_ref.shape[0]
    cols = heads * P_SIZE
    wide = cols + 2 * N
    place = place_ref[...]
    pre, step, step_t, log, log_t = decays(
        x_ref[:, wide:], place, bias_ref[...], bias_t_ref[...], rate_ref[...], rate_t_ref[...]
    )
    growth = jnp.exp(log)
    tail_exp = jnp.exp(log[size - 1 :] - log)
    tail = tail_exp * step
    inputs_b = act_ref[:, cols : cols + N]
    readout = act_ref[:, cols + N :]
    scores = dots(readout, inputs_b, ((1,), (1,)))
    left = lax.broadcasted_iota(jnp.int32, (size, 128), 1) < P_SIZE
    upper = lax.broadcasted_iota(jnp.int32, (128, 128), 0) < P_SIZE

    def through_conv(at, grad):
        here = x_ref[:, at : at + 128].astype(F32)
        before = before_ref[8:, at : at + 128].astype(F32)
        if is_first:
            before = jnp.zeros_like(before)
        taps = taps_ref[:, at : at + 128]
        conv, ext = convolve(before, here, taps, cbias_ref[:, at : at + 128])
        sig = jax.nn.sigmoid(conv)
        grad = grad * (sig * (1.0 + conv * (1.0 - sig)))
        start = 8 - (CONV - 1)
        rows = [jnp.sum(grad * ext[start + o : start + o + size], axis=0, keepdims=True) for o in range(CONV)]
        rows += [jnp.sum(grad, axis=0, keepdims=True), jnp.zeros((3, 128), F32)]
        conv_ref[:, at : at + 128] += jnp.concatenate(rows, axis=0)
        onward = jnp.concatenate([grad, after[:, at : at + 128]], axis=0)
        after[:, at : at + 128] = grad[:8]
        total = taps[CONV - 1 : CONV] * grad
        for o in range(CONV - 1):
            total = total + taps[o : o + 1] * onward[CONV - 1 - o : CONV - 1 - o + size]
        out_ref[:, at : at + 128] = total.astype(BF16)

    score_sum[...] = jnp.zeros_like(score_sum)
    in_grad[...] = jnp.zeros_like(in_grad)
    read_grad[...] = jnp.zeros_like(read_grad)
    for pair in range(heads // 2):
        at = pair * 128
        a, b = 2 * pair, 2 * pair + 1
        vals = act_ref[:, at : at + 128]
        vals_f = vals.astype(F32)
        grad = grad_ref[:, at : at + 128]
        grad_f = grad.astype(F32)
        starts = starts_ref[at : at + 128, :]
        starts_low = starts.astype(BF16)
        held = state[at : at + 128, :]
        held_low = held.astype(BF16)
        grown = grad_f * jnp.where(left, growth[:, a : a + 1], growth[:, b : b + 1])
        outer_low = grown.astype(BF16)
        outer = grown * dots(readout, starts_low, ((1,), (1,)))
        read_grad[...] += dots(outer_low, starts_low, ((1,), (0,)))
        tail_pair = jnp.where(left, tail[:, a : a + 1], tail[:, b : b + 1])
        low = (vals_f * tail_pair).astype(BF16)
        in_grad[...] += dots(low, held_low, ((1,), (0,)))
        low_grad = dots(inputs_b, held_low, ((1,), (1,)))
        tail_part = low_grad * vals_f
        product = grad_f * vals_f
        skip_grad_ref[:, at : at + 128] += jnp.sum(product, axis=0, keepdims=True)
        keep = jnp.where(upper, growth[size - 1 :, a : a + 1], growth[size - 1 :, b : b + 1])
        shared = jnp.sum(held * starts, axis=1, keepdims=True)
        state[at : at + 128, :] = dots(outer_low, readout, ((0,), (0,))) + keep * held
        base = skip_ref[:, at : at + 128] * grad_f + low_grad * tail_pair
        top = base[: size // 2]
        bottom = base[size // 2 :]
        for head, side in ((a, left), (b, jnp.logical_not(left))):
            own = jnp.where(side, grad, 0)
            tails[:, head : head + 1] = jnp.sum(jnp.where(side, tail_part, 0.0), axis=1, keepdims=True)
            rows = []
            sums = jnp.zeros((1, size), F32)
            for span in spans(size):
                first, last, seen = span
                mix_grad = dots(own[first:last], vals[:seen], ((1,), (1,)))
                decay = decay_of(log, log_t, head, span)
                steps = step_t[head : head + 1, :seen]
                some = scores[first:last, :seen]
                decayed = mix_grad * decay
                by_score = decayed * some
                score_sum[first:last, :seen] += decayed * steps
                rows.append(jnp.sum(by_score * steps, axis=1, keepdims=True))
                sums = sums + jnp.pad(jnp.sum(by_score, axis=0, keepdims=True), ((0, 0), (0, size - seen)))
                back = dots((some * decay * steps).astype(BF16), own[first:last], ((0,), (0,)))
                top = top + back[: size // 2]
                if seen == size:
                    bottom = bottom + back[size // 2 :]
            by_row[head : head + 1, :] = sums
            flow = jnp.sum(jnp.where(side, outer, 0.0), axis=1, keepdims=True)
            by_col[:, head : head + 1] = jnp.concatenate(rows, axis=0) + flow
            half = shared[:P_SIZE] if head == a else shared[P_SIZE:]
            by_col[size - 1 :, head : head + 1] += growth[size - 1 :, head : head + 1] * jnp.sum(
                half, axis=0, keepdims=True
            )
        through_conv(at, jnp.concatenate([top, bottom], axis=0))

    score_grad = score_sum[...].astype(BF16)
    through_conv(cols, in_grad[...] + dots(score_grad, readout, ((0,), (0,))))
    through_conv(cols + N, read_grad[...] + dots(score_grad, inputs_b, ((1,), (0,))))

    eye = (
        lax.broadcasted_iota(jnp.int32, (heads, heads), 0) == lax.broadcasted_iota(jnp.int32, (heads, heads), 1)
    ).astype(F32)
    summed = dots(by_row[...], eye, ((0,), (0,)), True)
    tail_grad = tails[...]
    tail_term = tail_grad * tail
    log_grad = by_col[...] - step * summed - tail_term
    row = lax.broadcasted_iota(jnp.int32, log_grad.shape, 0)
    log_grad = log_grad + jnp.where(row == size - 1, jnp.sum(tail_term, axis=0, keepdims=True), 0.0)
    decay_grad = dots(triangle(size, True), log_grad, ((1,), (0,)), True)
    step_grad = summed + tail_grad * tail_exp + decay_grad * rate_ref[...]
    raw = step_grad * jax.nn.sigmoid(pre)
    head_ref[...] += jnp.concatenate(
        [
            jnp.sum(raw, axis=0, keepdims=True),
            jnp.sum(decay_grad * step, axis=0, keepdims=True) * rate_ref[...],
            jnp.zeros((6, heads), F32),
        ],
        axis=0,
    )
    out_ref[:, wide:] = dots(raw.astype(BF16), place, ((1,), (0,))).astype(BF16)


def whole_spec(value):
    return pl.BlockSpec(value.shape, lambda k: (0,) * value.ndim)


def row_spec(value):
    return pl.BlockSpec((SPAN, value.shape[1]), lambda k: (k, 0))


def project_kernel(left_ref, *refs):
    *pieces, out_ref, whole = refs
    join(pieces, whole)
    out_ref[...] = dots(left_ref[...], whole[...], ((1,), (1,))).astype(BF16)


def run_project(left, pieces):
    out = jax.ShapeDtypeStruct((left.shape[0], pieces[0].shape[0]), BF16)
    return pl.pallas_call(
        project_kernel,
        grid=(left.shape[0] // TALL,),
        in_specs=[tall_spec(left)] + [whole_spec(p) for p in pieces],
        out_specs=tall_spec(out),
        out_shape=out,
        scratch_shapes=[joined(pieces)],
        compiler_params=pltpu.CompilerParams(dimension_semantics=("arbitrary",)),
        name="project",
    )(left, *pieces)


def run_scan_forward(x_proj, params):
    rows, width = x_proj.shape
    wide = params[0].shape[1]
    cols = wide - 2 * N
    blocks = rows // SPAN
    per = 2
    outs = [
        jax.ShapeDtypeStruct((rows, wide), BF16),
        jax.ShapeDtypeStruct((rows, cols), F32),
        jax.ShapeDtypeStruct((blocks * cols, N), F32),
    ]
    carried = [jax.ShapeDtypeStruct((8, wide), F32), jax.ShapeDtypeStruct((cols, N), F32)]
    held = None
    for at in range(0, blocks, per):
        args = [x_proj, *params]
        ins = [pl.BlockSpec((SPAN, width), lambda k, at=at: (at + k, 0))] + [whole_spec(p) for p in params]
        aliases = {}
        if held is not None:
            aliases = {len(args) + i: i for i in range(len(held))}
            ins += [pl.BlockSpec(memory_space=pl.ANY) for _ in outs] + [whole_spec(c) for c in carried]
            args += held
        held = pl.pallas_call(
            functools.partial(scan_forward, held is None),
            grid=(per,),
            in_specs=ins,
            out_specs=[
                pl.BlockSpec((SPAN, wide), lambda k, at=at: (at + k, 0)),
                pl.BlockSpec((SPAN, cols), lambda k, at=at: (at + k, 0)),
                pl.BlockSpec((cols, N), lambda k, at=at: (at + k, 0)),
            ]
            + [whole_spec(c) for c in carried],
            out_shape=outs + carried,
            input_output_aliases=aliases,
            compiler_params=pltpu.CompilerParams(dimension_semantics=("arbitrary",)),
        )(*args)
    return held[:3]


TALL = 2 * SPAN


def tall_spec(value):
    return pl.BlockSpec((TALL, value.shape[1]), lambda k: (k, 0))


def across_spec():
    return pl.BlockSpec((8, TALL), lambda k: (0, k))


def gate_kernel(*refs):
    normed_ref, mixed_ref, mask_ref, *pieces, gate_ref, square_ref, whole = refs
    join(pieces, whole)
    gate = dots(normed_ref[...], whole[...], ((1,), (1,))).astype(BF16)
    gate_ref[...] = gate
    gate = gate.astype(F32)
    gated = mixed_ref[...] * (gate * jax.nn.sigmoid(gate)) * mask_ref[...]
    square_ref[...] = row_of_sums(gated * gated)


def run_gate(normed, mixed, mask, pieces):
    rows, cols = mixed.shape
    return pl.pallas_call(
        gate_kernel,
        grid=(rows // TALL,),
        in_specs=[tall_spec(normed), tall_spec(mixed), whole_spec(mask)] + [whole_spec(p) for p in pieces],
        out_specs=[tall_spec(mixed), across_spec()],
        out_shape=[jax.ShapeDtypeStruct((rows, cols), BF16), jax.ShapeDtypeStruct((8, rows), F32)],
        scratch_shapes=[joined(pieces)],
        compiler_params=pltpu.CompilerParams(dimension_semantics=("arbitrary",)),
        name="gate_forward",
    )(normed, mixed, mask, *pieces)


def normalize_kernel(mixed_ref, gate_ref, scale_ref, gain_ref, out_ref):
    gate = gate_ref[...].astype(F32)
    gated = mixed_ref[...] * (gate * jax.nn.sigmoid(gate))
    out_ref[...] = (gated * scale_ref[...] * gain_ref[...]).astype(BF16)


def run_normalize(mixed, gate, scale, gain):
    return pl.pallas_call(
        normalize_kernel,
        grid=(mixed.shape[0] // SPAN,),
        in_specs=[row_spec(mixed), row_spec(gate), row_spec(scale), whole_spec(gain)],
        out_specs=row_spec(gate),
        out_shape=jax.ShapeDtypeStruct(gate.shape, BF16),
        name="normalize",
    )(mixed, gate, scale, gain)


def gate_grad_kernel(*refs):
    cot_ref, mixed_ref, gate_ref, scale_ref, gain_ref, mask_ref, *pieces, grad_ref, aligned_ref, norm_ref, whole = refs
    join(pieces, whole)
    grad = dots(cot_ref[...], whole[...], ((1,), (1,)))
    grad_ref[...] = grad
    gate = gate_ref[...].astype(F32)
    product = grad * (mixed_ref[...] * (gate * jax.nn.sigmoid(gate)) * mask_ref[...])
    aligned_ref[...] = row_of_sums(product * gain_ref[...])

    @pl.when(pl.program_id(0) == 0)
    def _():
        norm_ref[...] = jnp.zeros_like(norm_ref)

    norm_ref[...] += jnp.sum(product * scale_ref[...], axis=0, keepdims=True)


def run_gate_grad(cot, mixed, gate, scale, gain, mask, pieces):
    rows, cols = mixed.shape
    return pl.pallas_call(
        gate_grad_kernel,
        grid=(rows // TALL,),
        in_specs=[tall_spec(cot), tall_spec(mixed), tall_spec(gate), tall_spec(scale)]
        + [whole_spec(gain), whole_spec(mask)]
        + [whole_spec(p) for p in pieces],
        out_specs=[tall_spec(mixed), across_spec(), pl.BlockSpec((1, cols), lambda k: (0, 0))],
        out_shape=[
            jax.ShapeDtypeStruct((rows, cols), F32),
            jax.ShapeDtypeStruct((8, rows), F32),
            jax.ShapeDtypeStruct((1, cols), F32),
        ],
        scratch_shapes=[joined(pieces)],
        compiler_params=pltpu.CompilerParams(dimension_semantics=("arbitrary",)),
        name="gate_backward",
    )(cot, mixed, gate, scale, gain, mask, *pieces)


def run_products(lefts, piece_lists, against=None):
    rows = lefts[0].shape[0]
    count = len(lefts)
    number = len(piece_lists[0])
    wide = piece_lists[0][0].shape[1]
    flat = [piece for pieces in piece_lists for piece in pieces]
    others = [] if against is None else [against]

    def kernel(*refs):
        wholes = refs[-count:]
        other = refs[count + len(flat) : -count]
        total = None
        for at in range(count):
            join(refs[count + at * number : count + (at + 1) * number], wholes[at])
            part = dots(refs[at][...], wholes[at][...], ((1,), (0,)))
            total = part if total is None else total + part
        other[len(others)][...] = total.astype(BF16)
        if others:
            sums = jnp.sum(total * other[0][...].astype(F32), axis=0, keepdims=True)

            @pl.when(pl.program_id(0) == 0)
            def _():
                other[2][...] = sums

            @pl.when(pl.program_id(0) > 0)
            def _():
                other[2][...] += sums

    out = jax.ShapeDtypeStruct((rows, wide * number), BF16)
    sums = [jax.ShapeDtypeStruct((1, wide * number), F32)] * len(others)
    return pl.pallas_call(
        kernel,
        grid=(rows // TALL,),
        in_specs=[tall_spec(left) for left in lefts] + [whole_spec(p) for p in flat] + [tall_spec(o) for o in others],
        out_specs=[tall_spec(out)] + [whole_spec(total) for total in sums],
        out_shape=[out] + sums,
        scratch_shapes=[joined(pieces) for pieces in piece_lists],
        compiler_params=pltpu.CompilerParams(dimension_semantics=("arbitrary",)),
    )(*lefts, *flat, *others)


def run_scan_backward(x_proj, act, mixed_low, starts, params):
    rows, width = x_proj.shape
    wide = act.shape[1]
    cols = wide - 2 * N
    heads = cols // P_SIZE
    blocks = rows // SPAN
    carried = [
        jax.ShapeDtypeStruct((8, wide), F32),
        jax.ShapeDtypeStruct((cols, N), F32),
        jax.ShapeDtypeStruct((8, wide), F32),
        jax.ShapeDtypeStruct((1, cols), F32),
        jax.ShapeDtypeStruct((8, heads), F32),
    ]
    held = None
    for at in range(blocks - 1, -1, -1):
        ins = [
            pl.BlockSpec((SPAN, width), lambda k, at=at: (at, 0)),
            pl.BlockSpec((16, width), lambda k, at=at: (max(at * (SPAN // 16) - 1, 0), 0)),
            pl.BlockSpec((SPAN, wide), lambda k, at=at: (at, 0)),
            pl.BlockSpec((SPAN, cols), lambda k, at=at: (at, 0)),
            pl.BlockSpec((cols, N), lambda k, at=at: (at, 0)),
        ] + [whole_spec(p) for p in params]
        args = [x_proj, x_proj, act, mixed_low, starts, *params]
        aliases = {}
        if held is not None:
            aliases = {len(args) + i: i for i in range(len(held))}
            ins += [pl.BlockSpec(memory_space=pl.ANY)] + [whole_spec(c) for c in carried]
            args += held
        held = pl.pallas_call(
            functools.partial(scan_backward, held is None, at == 0),
            grid=(1,),
            in_specs=ins,
            out_specs=[pl.BlockSpec((SPAN, width), lambda k, at=at: (at, 0))] + [whole_spec(c) for c in carried],
            out_shape=[jax.ShapeDtypeStruct((rows, width), BF16)] + carried,
            input_output_aliases=aliases,
            scratch_shapes=[
                pltpu.VMEM((SPAN, heads), F32),
                pltpu.VMEM((heads, SPAN), F32),
                pltpu.VMEM((SPAN, heads), F32),
                pltpu.VMEM((SPAN, SPAN), F32),
                pltpu.VMEM((SPAN, N), F32),
                pltpu.VMEM((SPAN, N), F32),
            ],
        )(*args)
    return held[0], *held[3:]


def local(
    block_input,
    width_index,
    w_in,
    w_out,
    conv_weight,
    conv_bias,
    dt_bias,
    a_log,
    d_skip,
    norm_in_gain,
    norm_out_gain,
    out_cotangent,
):
    tok_rows, _ = block_input.shape
    inner = H * P_SIZE
    xbc = inner + 2 * N
    full_cols = 2 * inner + 2 * N + H
    groups, group = lax.axis_size("state"), lax.axis_index("state")
    seq_rows = tok_rows * groups
    heads = H // groups
    cols = inner // groups
    store = full_cols // groups

    def store_range(i):
        return (store * i, store * (i + 1))

    def value_range(i):
        return (inner + cols * i, inner + cols * (i + 1))

    def gate_range(i):
        return (cols * i, cols * (i + 1))

    def tail_range(i):
        return (inner + inner, full_cols)

    value_moves = moves(groups, store_range, value_range)
    tail_moves = moves(groups, store_range, tail_range)
    gate_moves = moves(groups, store_range, gate_range)

    def x_ranges(i):
        return [value_range(i), tail_range(i)]

    def at_shift(ranges, shift):
        return [ranges(g + shift) if 0 <= g + shift < groups else None for g in range(groups)]

    kinds = (("v", value_range, value_moves), ("b", tail_range, tail_moves), ("g", gate_range, gate_moves))
    sends = [(f"{kind}{abs(shift)}", ranges, shift, found[shift]) for kind, ranges, found in kinds for shift in sorted(found)]
    plans = [at_shift(x_ranges, 0), at_shift(lambda i: [gate_range(i)], 0)]
    plans += [at_shift(lambda i, ranges=ranges: [ranges(i)], shift) for _, ranges, shift, _ in sends]
    w_x_own, w_g_own, *cuts = cut_rows(w_in.T, group, plans)
    came = {"v": None, "b": None, "g": None}
    for (name, _, _, found), cut in zip(sends, cuts):
        part = lax.ppermute(cut, "state", found)
        came[name[0]] = part if came[name[0]] is None else came[name[0]] + part
    w_x_own = w_x_own + jnp.concatenate([came["v"], came["b"]], axis=0)
    w_g_own = w_g_own + came["g"]

    tokens = block_input.astype(F32)
    in_scale = lax.rsqrt(jnp.mean(tokens * tokens, axis=-1, keepdims=True) + EPSILON)
    normed = (tokens * in_scale * norm_in_gain).astype(BF16)

    w_x = gather_dp(w_x_own)
    normed_all = gather_state(to_ring(normed, "dp"))
    w_g = gather_dp(w_g_own)
    cot_all = gather_state(to_ring(out_cotangent, "dp"))
    w_o = gather_dp(w_out)

    own_heads = heads * group

    def own(entries, at, size):
        return lax.dynamic_slice_in_dim(entries, at, size, entries.ndim - 1)

    taps = jnp.concatenate([own(conv_weight, cols * group, cols), conv_weight[:, inner:]], axis=1)
    bias = jnp.concatenate([own(conv_bias, cols * group, cols), conv_bias[inner:]], axis=0)[None]
    gain_own = own(norm_out_gain, cols * group, cols)
    dt_own = own(dt_bias, own_heads, heads)
    rate_own = -jnp.exp(own(a_log, own_heads, heads))
    skip_own = jnp.repeat(own(d_skip, own_heads, heads), P_SIZE)[None]
    place = (own_heads + jnp.arange(heads)[:, None] == jnp.arange(H)[None, :]).astype(BF16)
    scan_params = (taps, bias, place, dt_own[None], dt_own[:, None], rate_own[None], rate_own[:, None], skip_own)
    x_proj = run_project(normed_all, w_x)
    act, mixed, starts = run_scan_forward(x_proj, scan_params)

    heads_on = H // 8 * jnp.left_shift(1, width_index[0])
    mask = ((cols * group + jnp.arange(cols)) // P_SIZE < heads_on).astype(F32)[None]
    active = (heads_on * P_SIZE).astype(F32)
    gain_mask = gain_own[None] * mask
    gate, square = run_gate(normed_all, mixed, mask, w_g)
    square = lax.psum(square[:1], "state")
    scale_row = lax.rsqrt(square / active + EPSILON)
    out_scale = scale_row.reshape(seq_rows, 1)
    normed_out = run_normalize(mixed, gate, out_scale, gain_mask)
    grad_out_proj = scatter_dp(normed_out, cot_all)

    out_grad, aligned, norm_sums = run_gate_grad(cot_all, mixed, gate, out_scale, gain_mask, mask, w_o)
    grad_norm_out = norm_sums[0]
    mixed, gate, out_grad = lax.optimization_barrier((mixed, gate, out_grad))
    gate_f = gate.astype(F32)
    gate_sig = jax.nn.sigmoid(gate_f)
    gate_act = gate_f * gate_sig
    gated = mixed * gate_act
    aligned = lax.psum(aligned[:1], "state").reshape(seq_rows, 1)
    pull = (aligned / active) * out_scale * out_scale * out_scale
    gated_grad = out_grad * gain_mask * out_scale - gated * mask * pull
    mixed_grad = gated_grad * gate_act
    gate_grad = (gated_grad * mixed * (gate_sig * (1.0 + gate_f * (1.0 - gate_sig)))).astype(BF16)

    (out_whole,) = run_products([normed_out], [w_o])
    block_out = (tokens + from_ring(scatter_state(out_whole), "dp")).astype(BF16)
    grad_in_gate = scatter_dp(gate_grad, normed_all)
    x_grad, conv_sums, skip_sums, head_sums = run_scan_backward(
        x_proj, act, mixed_grad.astype(BF16), starts, scan_params
    )
    taps_cols, bias_cols = conv_sums[:CONV], conv_sums[CONV]
    grad_d_skip = jnp.sum(skip_sums.reshape(heads, P_SIZE), axis=1)
    grad_dt_bias, grad_a_log = head_sums[0], head_sums[1]

    grad_in_x = scatter_dp(x_grad, normed_all)
    x_low, gate_low = grad_in_x.astype(BF16), grad_in_gate.astype(BF16)
    held = {"v": x_low[:cols], "b": x_low[cols:], "g": gate_low}
    pieces = [grad_in_x, grad_in_gate]
    plans = [at_shift(x_ranges, 0), at_shift(lambda i: [gate_range(i)], 0)]
    for name, ranges, shift, found in sends:
        pieces.append(lax.ppermute(held[name[0]], "state", [(b, a) for a, b in found]))
        plans.append(at_shift(lambda i, ranges=ranges: [ranges(i)], shift))
    grad_in_proj = paste_rows(pieces, group, plans, store).T

    normed_whole, gain_sums = run_products([x_grad, gate_grad], [w_x, w_g], normed_all)
    normed_grad = from_ring(scatter_state(normed_whole), "dp")
    pushed = normed_grad * norm_in_gain
    token_grad = in_scale * pushed - tokens * (
        in_scale * in_scale * in_scale * jnp.mean(pushed * tokens, axis=-1, keepdims=True)
    )
    grad_input = out_cotangent.astype(F32) + token_grad
    grad_norm_in = from_ring(gain_sums, "dp")[0] / norm_in_gain

    def spread(entries, total, at):
        return lax.dynamic_update_slice_in_dim(
            jnp.zeros(entries.shape[:-1] + (total,), F32), entries, at, entries.ndim - 1
        )

    taps_wide = spread(taps_cols[:, :cols], xbc, cols * group).at[:, inner:].set(taps_cols[:, cols:])
    bias_wide = spread(bias_cols[:cols], xbc, cols * group).at[inner:].set(bias_cols[cols:])
    flat = [
        taps_wide.reshape(-1),
        bias_wide,
        spread(grad_dt_bias, H, own_heads),
        spread(grad_a_log, H, own_heads),
        spread(grad_d_skip, H, own_heads),
        grad_norm_in,
        spread(grad_norm_out, inner, cols * group),
    ]
    sizes = [entry.shape[0] for entry in flat]
    packed = jnp.concatenate(flat)
    packed = jnp.pad(packed, (0, -packed.shape[0] % 1024)).reshape(-1, 128)
    packed = sum_axis(sum_axis(packed, "state"), "dp").reshape(-1)
    summed = []
    at = 0
    for size in sizes:
        summed.append(packed[at : at + size])
        at += size
    return (
        block_out,
        grad_input,
        grad_in_proj,
        grad_out_proj,
        summed[0].reshape(CONV, xbc),
        summed[1],
        summed[2],
        summed[3],
        summed[4],
        summed[5],
        summed[6],
    )


def solution(mesh):
    rows = P(("dp", "state"), None)
    whole = P()
    in_specs = (rows, P("dp"), P("dp", "state"), P("state", "dp")) + (whole,) * 7 + (rows,)
    out_specs = (rows, rows, P("dp", "state"), P("state", "dp")) + (whole,) * 7

    return jax.shard_map(local, mesh=mesh, in_specs=in_specs, out_specs=out_specs, check_vma=False)
```

```python
import functools

import jax
import jax.numpy as jnp
from jax import lax
from jax.experimental import pallas as pl
from jax.experimental.pallas import tpu as pltpu
from jax.sharding import PartitionSpec as P

H = 64
P_SIZE = 64
N = 128
SPAN = 256
CONV = 4
EPSILON = 1e-05
F32 = jnp.float32
BF16 = jnp.bfloat16
DP, STATE = "dp", "state"
IN_ORDER = pltpu.CompilerParams(dimension_semantics=("arbitrary",))


def flip(value, axis, bit):
    return lax.ppermute(value, axis, [(i, i ^ bit) for i in range(lax.axis_size(axis))])


def moves(count, from_range, to_range):
    found = {}
    for source in range(count):
        for target in range(count):
            a, b = from_range(source), to_range(target)
            if source != target and max(a[0], b[0]) < min(a[1], b[1]):
                found.setdefault(target - source, []).append((source, target))
    return found


def stack_rows(parts, places):
    rows, width = parts[0].shape

    def kernel(places_ref, *refs):
        out = refs[-1]
        for i, part in enumerate(refs[:-1]):
            out[pl.ds(pl.multiple_of(places_ref[i] * rows, rows), rows), :] = part[...]

    return pl.pallas_call(
        kernel,
        in_specs=[pl.BlockSpec(memory_space=pltpu.SMEM)]
        + [pl.BlockSpec(memory_space=pltpu.VMEM) for _ in parts],
        out_specs=pl.BlockSpec(memory_space=pltpu.VMEM),
        out_shape=jax.ShapeDtypeStruct((rows * len(parts), width), parts[0].dtype),
    )(places, *parts)


def gather_state(own):
    count, here = lax.axis_size(STATE), lax.axis_index(STATE)
    held = {0: own}
    bit = count // 2
    while bit:
        for key in list(held):
            held[key | bit] = flip(held[key], STATE, bit)
        bit //= 2
    keys = sorted(held)
    return stack_rows([held[key] for key in keys], here ^ jnp.array(keys))


def ringed(axis):
    return lax.axis_size(axis) <= 8


def to_ring(value, axis):
    if not ringed(axis):
        return value
    count, here = lax.axis_size(axis), lax.axis_index(axis)
    steps = count // 2
    pair = value.shape[1] // count
    sides = []
    for side in range(2):
        blocks = [value[:, (2 * i + side) * pair : (2 * i + side + 1) * pair] for i in range(steps)][::-1]
        turned = jnp.concatenate(blocks + blocks[:-1], axis=1)
        sides.append(lax.dynamic_slice_in_dim(turned, (steps - 1 - here // 2) * pair, steps * pair, 1))
    even = here % 2 == 0
    return jnp.concatenate([jnp.where(even, *sides), jnp.where(even, *sides[::-1])], axis=1)


def from_ring(value, axis):
    if not ringed(axis):
        return value
    count, here = lax.axis_size(axis), lax.axis_index(axis)
    steps = count // 2
    pair = value.shape[1] // count
    first, second = value[:, : steps * pair], value[:, steps * pair :]
    even = here % 2 == 0
    sides = []
    for side in (jnp.where(even, first, second), jnp.where(even, second, first)):
        blocks = [side[:, i * pair : (i + 1) * pair] for i in range(steps)][::-1]
        turned = jnp.concatenate(blocks + blocks[:-1], axis=1)
        sides.append(lax.dynamic_slice_in_dim(turned, (steps - 1 - here // 2) * pair, steps * pair, 1))
    return jnp.concatenate(
        [sides[i % 2][:, i // 2 * pair : (i // 2 + 1) * pair] for i in range(count)], axis=1
    )


def gather_dp(own):
    count = lax.axis_size(DP)
    if not ringed(DP):
        return [lax.all_gather(own, DP, axis=1, tiled=True)]
    ring = [(i, (i + 2) % count) for i in range(count)]
    mine, other = [own], []
    for step in range(count // 2):
        other.append(flip(mine[step], DP, 1))
        if step + 1 < count // 2:
            mine.append(lax.ppermute(mine[step], DP, ring))
    return mine + other


def scatter_dp(left, right):
    count = lax.axis_size(DP)

    def multiply(some, kind):
        return lax.dot_general(left, some, (((0,), (0,)), ((), ())), preferred_element_type=kind)

    if not ringed(DP):
        return lax.psum_scatter(multiply(right, F32), DP, scatter_dimension=1, tiled=True)
    steps = count // 2
    half = right.shape[1] // 2
    wide = half // steps
    ring = [(i, (i + 2) % count) for i in range(count)]
    other = multiply(right[:, half:], BF16)
    mine = multiply(right[:, :half], BF16)
    carried = None
    for step in range(1, steps + 1):
        at = step % steps * wide
        came = flip(other[:, at : at + wide], DP, 1)
        total = mine[:, at : at + wide].astype(F32) + came.astype(F32)
        if carried is not None:
            total = total + carried.astype(F32)
        if step < steps:
            carried = lax.ppermute(total.astype(BF16), DP, ring)
    return total


def scatter_state(whole):
    count, here = lax.axis_size(STATE), lax.axis_index(STATE)
    rows = whole.reshape(count, whole.shape[0] // count, whole.shape[1])
    parts = {key: lax.dynamic_index_in_dim(rows, here ^ key, 0, keepdims=False) for key in range(count)}
    bit = 1
    while bit < count:
        for key in [k for k in parts if not k & bit]:
            sent = flip(parts.pop(key | bit).astype(BF16), STATE, bit)
            parts[key] = parts[key].astype(F32) + sent.astype(F32)
        bit *= 2
    return parts[0]


def sum_axis(value, axis):
    bits = []
    while 1 << len(bits) < lax.axis_size(axis):
        bits.append(1 << len(bits))
    for bit in bits:
        value = value + flip(value, axis, bit)
    return value


def meet(first, second):
    low, high = max(first[0], second[0]), min(first[1], second[1])
    return (low, high) if low < high else None


def cut_rows(own, group, plans):
    groups = len(plans[0])
    store, width = own.shape
    sizes = [max(sum(b - a for a, b in ranges) for ranges in plan if ranges) for plan in plans]

    def kernel(group_ref, own_ref, *outs):
        for out in outs:
            out[...] = jnp.zeros_like(out)
        for g in range(groups):

            @pl.when(group_ref[0] == g)
            def _():
                for out, plan in zip(outs, plans):
                    at = 0
                    for ask in plan[g] or []:
                        found = meet(ask, (store * g, store * (g + 1)))
                        if found:
                            low, high = found
                            out[at + low - ask[0] : at + high - ask[0], :] = own_ref[low - store * g : high - store * g, :]
                        at += ask[1] - ask[0]

    return pl.pallas_call(
        kernel,
        in_specs=[pl.BlockSpec(memory_space=pltpu.SMEM), pl.BlockSpec(memory_space=pltpu.VMEM)],
        out_specs=[pl.BlockSpec(memory_space=pltpu.VMEM) for _ in plans],
        out_shape=[jax.ShapeDtypeStruct((size, width), BF16) for size in sizes],
        name="cut",
    )(group[None], own)


def paste_rows(pieces, group, plans, store):
    groups = len(plans[0])
    width = pieces[0].shape[1]

    def kernel(group_ref, *refs):
        out = refs[-1]
        out[...] = jnp.zeros_like(out)
        for g in range(groups):

            @pl.when(group_ref[0] == g)
            def _():
                for piece, plan in zip(refs[:-1], plans):
                    at = 0
                    for ask in plan[g] or []:
                        found = meet(ask, (store * g, store * (g + 1)))
                        if found:
                            low, high = found
                            out[low - store * g : high - store * g, :] += piece[
                                at + low - ask[0] : at + high - ask[0], :
                            ].astype(F32)
                        at += ask[1] - ask[0]

    return pl.pallas_call(
        kernel,
        in_specs=[pl.BlockSpec(memory_space=pltpu.SMEM)]
        + [pl.BlockSpec(memory_space=pltpu.VMEM) for _ in pieces],
        out_specs=pl.BlockSpec(memory_space=pltpu.VMEM),
        out_shape=jax.ShapeDtypeStruct((store, width), F32),
        name="paste",
    )(group[None], *pieces)


def spans(size):
    half = size // 2
    return [(0, half, half), (half, size, size)]


def dots(left, right, contract, exact=False):
    return lax.dot_general(
        left,
        right,
        (contract, ((), ())),
        preferred_element_type=F32,
        precision=lax.Precision.HIGHEST if exact else None,
    )


def softplus(value):
    return jnp.maximum(value, 0.0) + jnp.log1p(jnp.exp(-jnp.abs(value)))


def triangle(size, upper):
    row = lax.broadcasted_iota(jnp.int32, (size, size), 0)
    col = lax.broadcasted_iota(jnp.int32, (size, size), 1)
    return (row <= col if upper else row >= col).astype(F32)


def decays(raw, place, bias, bias_t, rate, rate_t):
    pre = dots(raw, place, ((1,), (1,))) + bias
    pre_t = dots(place, raw, ((1,), (1,))) + bias_t
    step, step_t = softplus(pre), softplus(pre_t)
    size = raw.shape[0]
    log = dots(triangle(size, False), step * rate, ((1,), (0,)), True)
    log_t = dots(step_t * rate_t, triangle(size, True), ((1,), (0,)), True)
    return pre, step, step_t, log, log_t


def decay_of(log, log_t, head, span):
    first, last, seen = span
    gap = log[first:last, head : head + 1] - log_t[head : head + 1, :seen]
    row = first + lax.broadcasted_iota(jnp.int32, gap.shape, 0)
    col = lax.broadcasted_iota(jnp.int32, gap.shape, 1)
    return jnp.exp(jnp.where(row >= col, gap, -jnp.inf))


def convolve(before, here, taps, bias):
    ext = jnp.concatenate([before, here], axis=0)
    size = here.shape[0]
    start = before.shape[0] - (CONV - 1)
    total = bias + taps[0:1] * ext[start : start + size]
    for offset in range(1, CONV):
        total = total + taps[offset : offset + 1] * ext[start + offset : start + offset + size]
    return total, ext


def join(pieces, whole):
    @pl.when(pl.program_id(0) == 0)
    def _():
        wide = pieces[0].shape[1]
        for i, piece in enumerate(pieces):
            whole[:, i * wide : (i + 1) * wide] = piece[...]


def joined(pieces):
    return pltpu.VMEM((pieces[0].shape[0], sum(p.shape[1] for p in pieces)), BF16)


def row_of_sums(value):
    total = value[:, :128]
    for at in range(128, value.shape[1], 128):
        total = total + value[:, at : at + 128]
    return dots(jnp.ones((8, 128), F32), total, ((1,), (1,)), True)


def scan_forward(is_first, *refs):
    x_ref, taps_ref, cbias_ref, place_ref, bias_ref, bias_t_ref, rate_ref, rate_t_ref, skip_ref = refs[:9]
    act_ref, mixed_ref, starts_ref, halo, state = refs[-5:]

    @pl.when(pl.program_id(0) == 0)
    def _():
        for new, old in zip((halo, state), refs[-7:-5]):
            new[...] = jnp.zeros_like(new) if is_first else old[...]

    size = x_ref.shape[0]
    heads = place_ref.shape[0]
    cols = heads * P_SIZE
    wide = cols + 2 * N
    for at in range(0, wide, 128):
        here = x_ref[:, at : at + 128].astype(F32)
        conv, _ = convolve(halo[:, at : at + 128], here, taps_ref[:, at : at + 128], cbias_ref[:, at : at + 128])
        act_ref[:, at : at + 128] = (conv * jax.nn.sigmoid(conv)).astype(BF16)
        halo[:, at : at + 128] = here[size - 8 :]
    _, step, step_t, log, log_t = decays(
        x_ref[:, wide:], place_ref[...], bias_ref[...], bias_t_ref[...], rate_ref[...], rate_t_ref[...]
    )
    growth = jnp.exp(log)
    tail = jnp.exp(log[size - 1 :] - log) * step
    inputs_b = act_ref[:, cols : cols + N]
    readout = act_ref[:, cols + N :]
    scores = dots(readout, inputs_b, ((1,), (1,)))
    left = lax.broadcasted_iota(jnp.int32, (size, 128), 1) < P_SIZE
    upper = lax.broadcasted_iota(jnp.int32, (128, 128), 0) < P_SIZE
    for pair in range(heads // 2):
        at = pair * 128
        a, b = 2 * pair, 2 * pair + 1
        vals = act_ref[:, at : at + 128]
        vals_f = vals.astype(F32)
        held = state[at : at + 128, :]
        starts_ref[at : at + 128, :] = held
        outer = dots(readout, held.astype(BF16), ((1,), (1,)))
        base = jnp.where(left, growth[:, a : a + 1], growth[:, b : b + 1]) * outer + skip_ref[:, at : at + 128] * vals_f
        split = [jnp.where(left, vals, 0), jnp.where(left, 0, vals)]
        for span in spans(size):
            first, last, seen = span
            total = base[first:last]
            for head, part in ((a, split[0]), (b, split[1])):
                mix = scores[first:last, :seen] * decay_of(log, log_t, head, span) * step_t[head : head + 1, :seen]
                total = total + dots(mix.astype(BF16), part[:seen], ((1,), (0,)))
            mixed_ref[first:last, at : at + 128] = total
        low = (vals_f * jnp.where(left, tail[:, a : a + 1], tail[:, b : b + 1])).astype(BF16)
        keep = jnp.where(upper, growth[size - 1 :, a : a + 1], growth[size - 1 :, b : b + 1])
        state[at : at + 128, :] = keep * held + dots(low, inputs_b, ((0,), (0,)))


def scan_backward(is_last, is_first, *refs):
    (
        x_ref, before_ref, act_ref, grad_ref, starts_ref,
        taps_ref, cbias_ref, place_ref, bias_ref, bias_t_ref, rate_ref, rate_t_ref, skip_ref,
    ) = refs[:13]
    olds = refs[13:-12]
    out_ref, *news = refs[-12:-6]
    by_col, by_row, tails, score_sum, in_grad, read_grad = refs[-6:]
    for i, new in enumerate(news):
        new[...] = jnp.zeros_like(new) if is_last else olds[i + 1][...]
    after, state, conv_ref, skip_grad_ref, head_ref = news
    size = x_ref.shape[0]
    heads = place_ref.shape[0]
    cols = heads * P_SIZE
    wide = cols + 2 * N
    place = place_ref[...]
    pre, step, step_t, log, log_t = decays(
        x_ref[:, wide:], place, bias_ref[...], bias_t_ref[...], rate_ref[...], rate_t_ref[...]
    )
    growth = jnp.exp(log)
    tail_exp = jnp.exp(log[size - 1 :] - log)
    tail = tail_exp * step
    inputs_b = act_ref[:, cols : cols + N]
    readout = act_ref[:, cols + N :]
    scores = dots(readout, inputs_b, ((1,), (1,)))
    left = lax.broadcasted_iota(jnp.int32, (size, 128), 1) < P_SIZE
    upper = lax.broadcasted_iota(jnp.int32, (128, 128), 0) < P_SIZE

    def through_conv(at, grad):
        here = x_ref[:, at : at + 128].astype(F32)
        before = before_ref[8:, at : at + 128].astype(F32)
        if is_first:
            before = jnp.zeros_like(before)
        taps = taps_ref[:, at : at + 128]
        conv, ext = convolve(before, here, taps, cbias_ref[:, at : at + 128])
        sig = jax.nn.sigmoid(conv)
        grad = grad * (sig * (1.0 + conv * (1.0 - sig)))
        start = 8 - (CONV - 1)
        rows = [jnp.sum(grad * ext[start + o : start + o + size], axis=0, keepdims=True) for o in range(CONV)]
        rows += [jnp.sum(grad, axis=0, keepdims=True), jnp.zeros((3, 128), F32)]
        conv_ref[:, at : at + 128] += jnp.concatenate(rows, axis=0)
        onward = jnp.concatenate([grad, after[:, at : at + 128]], axis=0)
        after[:, at : at + 128] = grad[:8]
        total = taps[CONV - 1 : CONV] * grad
        for o in range(CONV - 1):
            total = total + taps[o : o + 1] * onward[CONV - 1 - o : CONV - 1 - o + size]
        out_ref[:, at : at + 128] = total.astype(BF16)

    score_sum[...] = jnp.zeros_like(score_sum)
    in_grad[...] = jnp.zeros_like(in_grad)
    read_grad[...] = jnp.zeros_like(read_grad)
    for pair in range(heads // 2):
        at = pair * 128
        a, b = 2 * pair, 2 * pair + 1
        vals = act_ref[:, at : at + 128]
        vals_f = vals.astype(F32)
        grad = grad_ref[:, at : at + 128]
        grad_f = grad.astype(F32)
        starts = starts_ref[at : at + 128, :]
        starts_low = starts.astype(BF16)
        held = state[at : at + 128, :]
        held_low = held.astype(BF16)
        grown = grad_f * jnp.where(left, growth[:, a : a + 1], growth[:, b : b + 1])
        outer_low = grown.astype(BF16)
        outer = grown * dots(readout, starts_low, ((1,), (1,)))
        read_grad[...] += dots(outer_low, starts_low, ((1,), (0,)))
        tail_pair = jnp.where(left, tail[:, a : a + 1], tail[:, b : b + 1])
        low = (vals_f * tail_pair).astype(BF16)
        in_grad[...] += dots(low, held_low, ((1,), (0,)))
        low_grad = dots(inputs_b, held_low, ((1,), (1,)))
        tail_part = low_grad * vals_f
        product = grad_f * vals_f
        skip_grad_ref[:, at : at + 128] += jnp.sum(product, axis=0, keepdims=True)
        keep = jnp.where(upper, growth[size - 1 :, a : a + 1], growth[size - 1 :, b : b + 1])
        shared = jnp.sum(held * starts, axis=1, keepdims=True)
        state[at : at + 128, :] = dots(outer_low, readout, ((0,), (0,))) + keep * held
        base = skip_ref[:, at : at + 128] * grad_f + low_grad * tail_pair
        top = base[: size // 2]
        bottom = base[size // 2 :]
        for head, side in ((a, left), (b, jnp.logical_not(left))):
            own = jnp.where(side, grad, 0)
            tails[:, head : head + 1] = jnp.sum(jnp.where(side, tail_part, 0.0), axis=1, keepdims=True)
            rows = []
            sums = jnp.zeros((1, size), F32)
            for span in spans(size):
                first, last, seen = span
                mix_grad = dots(own[first:last], vals[:seen], ((1,), (1,)))
                decay = decay_of(log, log_t, head, span)
                steps = step_t[head : head + 1, :seen]
                some = scores[first:last, :seen]
                decayed = mix_grad * decay
                by_score = decayed * some
                score_sum[first:last, :seen] += decayed * steps
                rows.append(jnp.sum(by_score * steps, axis=1, keepdims=True))
                sums = sums + jnp.pad(jnp.sum(by_score, axis=0, keepdims=True), ((0, 0), (0, size - seen)))
                back = dots((some * decay * steps).astype(BF16), own[first:last], ((0,), (0,)))
                top = top + back[: size // 2]
                if seen == size:
                    bottom = bottom + back[size // 2 :]
            by_row[head : head + 1, :] = sums
            flow = jnp.sum(jnp.where(side, outer, 0.0), axis=1, keepdims=True)
            by_col[:, head : head + 1] = jnp.concatenate(rows, axis=0) + flow
            half = shared[:P_SIZE] if head == a else shared[P_SIZE:]
            by_col[size - 1 :, head : head + 1] += growth[size - 1 :, head : head + 1] * jnp.sum(
                half, axis=0, keepdims=True
            )
        through_conv(at, jnp.concatenate([top, bottom], axis=0))

    score_grad = score_sum[...].astype(BF16)
    through_conv(cols, in_grad[...] + dots(score_grad, readout, ((0,), (0,))))
    through_conv(cols + N, read_grad[...] + dots(score_grad, inputs_b, ((1,), (0,))))

    eye = (
        lax.broadcasted_iota(jnp.int32, (heads, heads), 0) == lax.broadcasted_iota(jnp.int32, (heads, heads), 1)
    ).astype(F32)
    summed = dots(by_row[...], eye, ((0,), (0,)), True)
    tail_grad = tails[...]
    tail_term = tail_grad * tail
    log_grad = by_col[...] - step * summed - tail_term
    row = lax.broadcasted_iota(jnp.int32, log_grad.shape, 0)
    log_grad = log_grad + jnp.where(row == size - 1, jnp.sum(tail_term, axis=0, keepdims=True), 0.0)
    decay_grad = dots(triangle(size, True), log_grad, ((1,), (0,)), True)
    step_grad = summed + tail_grad * tail_exp + decay_grad * rate_ref[...]
    raw = step_grad * jax.nn.sigmoid(pre)
    head_ref[...] += jnp.concatenate(
        [
            jnp.sum(raw, axis=0, keepdims=True),
            jnp.sum(decay_grad * step, axis=0, keepdims=True) * rate_ref[...],
            jnp.zeros((6, heads), F32),
        ],
        axis=0,
    )
    out_ref[:, wide:] = dots(raw.astype(BF16), place, ((1,), (0,))).astype(BF16)


def whole_spec(value):
    return pl.BlockSpec(value.shape, lambda k: (0,) * value.ndim)


def row_spec(value):
    return pl.BlockSpec((SPAN, value.shape[1]), lambda k: (k, 0))


def project_kernel(left_ref, *refs):
    *pieces, out_ref, whole = refs
    join(pieces, whole)
    out_ref[...] = dots(left_ref[...], whole[...], ((1,), (1,))).astype(BF16)


def run_project(left, pieces):
    out = jax.ShapeDtypeStruct((left.shape[0], pieces[0].shape[0]), BF16)
    return pl.pallas_call(
        project_kernel,
        grid=(left.shape[0] // TALL,),
        in_specs=[tall_spec(left)] + [whole_spec(p) for p in pieces],
        out_specs=tall_spec(out),
        out_shape=out,
        scratch_shapes=[joined(pieces)],
        compiler_params=IN_ORDER,
        name="pj",
    )(left, *pieces)


def run_scan_forward(x_proj, params):
    rows, width = x_proj.shape
    wide = params[0].shape[1]
    cols = wide - 2 * N
    blocks = rows // SPAN
    per = 2
    outs = [
        jax.ShapeDtypeStruct((rows, wide), BF16),
        jax.ShapeDtypeStruct((rows, cols), F32),
        jax.ShapeDtypeStruct((blocks * cols, N), F32),
    ]
    carried = [jax.ShapeDtypeStruct((8, wide), F32), jax.ShapeDtypeStruct((cols, N), F32)]
    held = None
    for at in range(0, blocks, per):
        args = [x_proj, *params]
        ins = [pl.BlockSpec((SPAN, width), lambda k, at=at: (at + k, 0))] + [whole_spec(p) for p in params]
        aliases = {}
        if held is not None:
            aliases = {len(args) + i: i for i in range(len(held))}
            ins += [pl.BlockSpec(memory_space=pl.ANY) for _ in outs] + [whole_spec(c) for c in carried]
            args += held
        held = pl.pallas_call(
            functools.partial(scan_forward, held is None),
            grid=(per,),
            in_specs=ins,
            out_specs=[
                pl.BlockSpec((SPAN, wide), lambda k, at=at: (at + k, 0)),
                pl.BlockSpec((SPAN, cols), lambda k, at=at: (at + k, 0)),
                pl.BlockSpec((cols, N), lambda k, at=at: (at + k, 0)),
            ]
            + [whole_spec(c) for c in carried],
            out_shape=outs + carried,
            input_output_aliases=aliases,
            compiler_params=IN_ORDER,
        )(*args)
    return held[:3]


TALL = 2 * SPAN


def tall_spec(value):
    return pl.BlockSpec((TALL, value.shape[1]), lambda k: (k, 0))


def across_spec():
    return pl.BlockSpec((8, TALL), lambda k: (0, k))


def gate_kernel(*refs):
    normed_ref, mixed_ref, mask_ref, *pieces, gate_ref, square_ref, whole = refs
    join(pieces, whole)
    gate = dots(normed_ref[...], whole[...], ((1,), (1,))).astype(BF16)
    gate_ref[...] = gate
    gate = gate.astype(F32)
    gated = mixed_ref[...] * (gate * jax.nn.sigmoid(gate)) * mask_ref[...]
    square_ref[...] = row_of_sums(gated * gated)


def run_gate(normed, mixed, mask, pieces):
    rows, cols = mixed.shape
    return pl.pallas_call(
        gate_kernel,
        grid=(rows // TALL,),
        in_specs=[tall_spec(normed), tall_spec(mixed), whole_spec(mask)] + [whole_spec(p) for p in pieces],
        out_specs=[tall_spec(mixed), across_spec()],
        out_shape=[jax.ShapeDtypeStruct((rows, cols), BF16), jax.ShapeDtypeStruct((8, rows), F32)],
        scratch_shapes=[joined(pieces)],
        compiler_params=IN_ORDER,
        name="gf",
    )(normed, mixed, mask, *pieces)


def normalize_kernel(mixed_ref, gate_ref, scale_ref, gain_ref, out_ref):
    gate = gate_ref[...].astype(F32)
    gated = mixed_ref[...] * (gate * jax.nn.sigmoid(gate))
    out_ref[...] = (gated * scale_ref[...] * gain_ref[...]).astype(BF16)


def run_normalize(mixed, gate, scale, gain):
    return pl.pallas_call(
        normalize_kernel,
        grid=(mixed.shape[0] // SPAN,),
        in_specs=[row_spec(mixed), row_spec(gate), row_spec(scale), whole_spec(gain)],
        out_specs=row_spec(gate),
        out_shape=jax.ShapeDtypeStruct(gate.shape, BF16),
        name="nr",
    )(mixed, gate, scale, gain)


def gate_grad_kernel(*refs):
    cot_ref, mixed_ref, gate_ref, scale_ref, gain_ref, mask_ref, *pieces, grad_ref, aligned_ref, norm_ref, whole = refs
    join(pieces, whole)
    grad = dots(cot_ref[...], whole[...], ((1,), (1,)))
    grad_ref[...] = grad
    gate = gate_ref[...].astype(F32)
    product = grad * (mixed_ref[...] * (gate * jax.nn.sigmoid(gate)) * mask_ref[...])
    aligned_ref[...] = row_of_sums(product * gain_ref[...])

    @pl.when(pl.program_id(0) == 0)
    def _():
        norm_ref[...] = jnp.zeros_like(norm_ref)

    norm_ref[...] += jnp.sum(product * scale_ref[...], axis=0, keepdims=True)


def run_gate_grad(cot, mixed, gate, scale, gain, mask, pieces):
    rows, cols = mixed.shape
    return pl.pallas_call(
        gate_grad_kernel,
        grid=(rows // TALL,),
        in_specs=[tall_spec(cot), tall_spec(mixed), tall_spec(gate), tall_spec(scale)]
        + [whole_spec(gain), whole_spec(mask)]
        + [whole_spec(p) for p in pieces],
        out_specs=[tall_spec(mixed), across_spec(), pl.BlockSpec((1, cols), lambda k: (0, 0))],
        out_shape=[
            jax.ShapeDtypeStruct((rows, cols), F32),
            jax.ShapeDtypeStruct((8, rows), F32),
            jax.ShapeDtypeStruct((1, cols), F32),
        ],
        scratch_shapes=[joined(pieces)],
        compiler_params=IN_ORDER,
        name="gb",
    )(cot, mixed, gate, scale, gain, mask, *pieces)


def run_products(left, pieces, onto=None, against=None):
    rows = left.shape[0]
    others = [] if onto is None else [onto, against]

    def kernel(left_ref, *refs):
        join(refs[: len(pieces)], refs[-1])
        total = dots(left_ref[...], refs[-1][...], ((1,), (0,)))
        if others:
            onto_ref, against_ref, out_ref, sums_ref = refs[len(pieces) : -1]
            total = total + onto_ref[...].astype(F32)
            sums = jnp.sum(total * against_ref[...].astype(F32), axis=0, keepdims=True)

            @pl.when(pl.program_id(0) == 0)
            def _():
                sums_ref[...] = sums

            @pl.when(pl.program_id(0) > 0)
            def _():
                sums_ref[...] += sums

        else:
            out_ref = refs[-2]
        out_ref[...] = total.astype(BF16)

    whole = joined(pieces)
    out = jax.ShapeDtypeStruct((rows, whole.shape[1]), BF16)
    sums = [jax.ShapeDtypeStruct((1, whole.shape[1]), F32)] if others else []
    return pl.pallas_call(
        kernel,
        grid=(rows // TALL,),
        in_specs=[tall_spec(left)] + [whole_spec(p) for p in pieces] + [tall_spec(o) for o in others],
        out_specs=[tall_spec(out)] + [whole_spec(total) for total in sums],
        out_shape=[out] + sums,
        scratch_shapes=[whole],
        compiler_params=IN_ORDER,
    )(left, *pieces, *others)


def run_scan_backward(x_proj, act, mixed_low, starts, params):
    rows, width = x_proj.shape
    wide = act.shape[1]
    cols = wide - 2 * N
    heads = cols // P_SIZE
    blocks = rows // SPAN
    carried = [
        jax.ShapeDtypeStruct((8, wide), F32),
        jax.ShapeDtypeStruct((cols, N), F32),
        jax.ShapeDtypeStruct((8, wide), F32),
        jax.ShapeDtypeStruct((1, cols), F32),
        jax.ShapeDtypeStruct((8, heads), F32),
    ]
    held = None
    for at in range(blocks - 1, -1, -1):
        ins = [
            pl.BlockSpec((SPAN, width), lambda k, at=at: (at, 0)),
            pl.BlockSpec((16, width), lambda k, at=at: (max(at * (SPAN // 16) - 1, 0), 0)),
            pl.BlockSpec((SPAN, wide), lambda k, at=at: (at, 0)),
            pl.BlockSpec((SPAN, cols), lambda k, at=at: (at, 0)),
            pl.BlockSpec((cols, N), lambda k, at=at: (at, 0)),
        ] + [whole_spec(p) for p in params]
        args = [x_proj, x_proj, act, mixed_low, starts, *params]
        aliases = {}
        if held is not None:
            aliases = {len(args) + i: i for i in range(len(held))}
            ins += [pl.BlockSpec(memory_space=pl.ANY)] + [whole_spec(c) for c in carried]
            args += held
        held = pl.pallas_call(
            functools.partial(scan_backward, held is None, at == 0),
            grid=(1,),
            in_specs=ins,
            out_specs=[pl.BlockSpec((SPAN, width), lambda k, at=at: (at, 0))] + [whole_spec(c) for c in carried],
            out_shape=[jax.ShapeDtypeStruct((rows, width), BF16)] + carried,
            input_output_aliases=aliases,
            scratch_shapes=[
                pltpu.VMEM((SPAN, heads), F32),
                pltpu.VMEM((heads, SPAN), F32),
                pltpu.VMEM((SPAN, heads), F32),
                pltpu.VMEM((SPAN, SPAN), F32),
                pltpu.VMEM((SPAN, N), F32),
                pltpu.VMEM((SPAN, N), F32),
            ],
        )(*args)
    return held[0], *held[3:]


def local(
    block_input,
    width_index,
    w_in,
    w_out,
    conv_weight,
    conv_bias,
    dt_bias,
    a_log,
    d_skip,
    norm_in_gain,
    norm_out_gain,
    out_cotangent,
):
    tok_rows, _ = block_input.shape
    inner = H * P_SIZE
    xbc = inner + 2 * N
    full_cols = 2 * inner + 2 * N + H
    groups, group = lax.axis_size(STATE), lax.axis_index(STATE)
    seq_rows = tok_rows * groups
    heads = H // groups
    cols = inner // groups
    store = full_cols // groups

    def store_range(i):
        return (store * i, store * (i + 1))

    def value_range(i):
        return (inner + cols * i, inner + cols * (i + 1))

    def gate_range(i):
        return (cols * i, cols * (i + 1))

    def tail_range(i):
        return (inner + inner, full_cols)

    value_moves = moves(groups, store_range, value_range)
    tail_moves = moves(groups, store_range, tail_range)
    gate_moves = moves(groups, store_range, gate_range)

    def x_ranges(i):
        return [value_range(i), tail_range(i)]

    def at_shift(ranges, shift):
        return [ranges(g + shift) if 0 <= g + shift < groups else None for g in range(groups)]

    kinds = (("v", value_range, value_moves), ("b", tail_range, tail_moves), ("g", gate_range, gate_moves))
    sends = [(kind + str(abs(shift)), ranges, shift, found[shift]) for kind, ranges, found in kinds for shift in sorted(found)]
    plans = [at_shift(x_ranges, 0), at_shift(lambda i: [gate_range(i)], 0)]
    plans += [at_shift(lambda i, ranges=ranges: [ranges(i)], shift) for _, ranges, shift, _ in sends]
    w_x_own, w_g_own, *cuts = cut_rows(w_in.T, group, plans)
    came = {"v": None, "b": None, "g": None}
    for (name, _, _, found), cut in zip(sends, cuts):
        part = lax.ppermute(cut, STATE, found)
        came[name[0]] = part if came[name[0]] is None else came[name[0]] + part
    w_x_own = w_x_own + jnp.concatenate([came["v"], came["b"]], axis=0)
    w_g_own = w_g_own + came["g"]

    tokens = block_input.astype(F32)
    in_scale = lax.rsqrt(jnp.mean(tokens * tokens, axis=-1, keepdims=True) + EPSILON)
    normed = (tokens * in_scale * norm_in_gain).astype(BF16)

    w_x = gather_dp(w_x_own)
    normed_all = gather_state(to_ring(normed, DP))
    w_g = gather_dp(w_g_own)
    cot_all = gather_state(to_ring(out_cotangent, DP))
    w_o = gather_dp(w_out)

    own_heads = heads * group

    def own(entries, at, size):
        return lax.dynamic_slice_in_dim(entries, at, size, entries.ndim - 1)

    taps = jnp.concatenate([own(conv_weight, cols * group, cols), conv_weight[:, inner:]], axis=1)
    bias = jnp.concatenate([own(conv_bias, cols * group, cols), conv_bias[inner:]], axis=0)[None]
    gain_own = own(norm_out_gain, cols * group, cols)
    dt_own = own(dt_bias, own_heads, heads)
    rate_own = -jnp.exp(own(a_log, own_heads, heads))
    skip_own = jnp.repeat(own(d_skip, own_heads, heads), P_SIZE)[None]
    place = (own_heads + jnp.arange(heads)[:, None] == jnp.arange(H)[None, :]).astype(BF16)
    scan_params = (taps, bias, place, dt_own[None], dt_own[:, None], rate_own[None], rate_own[:, None], skip_own)
    x_proj = run_project(normed_all, w_x)
    act, mixed, starts = run_scan_forward(x_proj, scan_params)

    heads_on = H // 8 * jnp.left_shift(1, width_index[0])
    mask = ((cols * group + jnp.arange(cols)) // P_SIZE < heads_on).astype(F32)[None]
    active = (heads_on * P_SIZE).astype(F32)
    gain_mask = gain_own[None] * mask
    gate, square = run_gate(normed_all, mixed, mask, w_g)
    square = lax.psum(square[:1], STATE)
    scale_row = lax.rsqrt(square / active + EPSILON)
    out_scale = scale_row.reshape(seq_rows, 1)
    normed_out = run_normalize(mixed, gate, out_scale, gain_mask)
    grad_out_proj = scatter_dp(normed_out, cot_all)

    out_grad, aligned, norm_sums = run_gate_grad(cot_all, mixed, gate, out_scale, gain_mask, mask, w_o)
    grad_norm_out = norm_sums[0]
    mixed, gate, out_grad = lax.optimization_barrier((mixed, gate, out_grad))
    gate_f = gate.astype(F32)
    gate_sig = jax.nn.sigmoid(gate_f)
    gate_act = gate_f * gate_sig
    gated = mixed * gate_act
    aligned = lax.psum(aligned[:1], STATE).reshape(seq_rows, 1)
    pull = (aligned / active) * out_scale * out_scale * out_scale
    gated_grad = out_grad * gain_mask * out_scale - gated * mask * pull
    mixed_grad = gated_grad * gate_act
    gate_grad = (gated_grad * mixed * (gate_sig * (1.0 + gate_f * (1.0 - gate_sig)))).astype(BF16)

    (out_whole,) = run_products(normed_out, w_o)
    block_out = (tokens + from_ring(scatter_state(out_whole), DP)).astype(BF16)
    grad_in_gate = scatter_dp(gate_grad, normed_all)
    x_grad, conv_sums, skip_sums, head_sums = run_scan_backward(
        x_proj, act, mixed_grad.astype(BF16), starts, scan_params
    )
    taps_cols, bias_cols = conv_sums[:CONV], conv_sums[CONV]
    grad_d_skip = jnp.sum(skip_sums.reshape(heads, P_SIZE), axis=1)
    grad_dt_bias, grad_a_log = head_sums[0], head_sums[1]

    grad_in_x = scatter_dp(x_grad, normed_all)
    x_low, gate_low = grad_in_x.astype(BF16), grad_in_gate.astype(BF16)
    held = {"v": x_low[:cols], "b": x_low[cols:], "g": gate_low}
    pieces = [grad_in_x, grad_in_gate]
    plans = [at_shift(x_ranges, 0), at_shift(lambda i: [gate_range(i)], 0)]
    for name, ranges, shift, found in sends:
        pieces.append(lax.ppermute(held[name[0]], STATE, [(b, a) for a, b in found]))
        plans.append(at_shift(lambda i, ranges=ranges: [ranges(i)], shift))
    grad_in_proj = paste_rows(pieces, group, plans, store).T

    (normed_x,) = run_products(x_grad, w_x)
    normed_whole, gain_sums = run_products(gate_grad, w_g, normed_x, normed_all)
    normed_grad = from_ring(scatter_state(normed_whole), DP)
    pushed = normed_grad * norm_in_gain
    token_grad = in_scale * pushed - tokens * (
        in_scale * in_scale * in_scale * jnp.mean(pushed * tokens, axis=-1, keepdims=True)
    )
    grad_input = out_cotangent.astype(F32) + token_grad
    grad_norm_in = from_ring(gain_sums, DP)[0] / norm_in_gain

    def spread(entries, total, at):
        return lax.dynamic_update_slice_in_dim(
            jnp.zeros(entries.shape[:-1] + (total,), F32), entries, at, entries.ndim - 1
        )

    taps_wide = spread(taps_cols[:, :cols], xbc, cols * group).at[:, inner:].set(taps_cols[:, cols:])
    bias_wide = spread(bias_cols[:cols], xbc, cols * group).at[inner:].set(bias_cols[cols:])
    flat = [
        taps_wide.reshape(-1),
        bias_wide,
        spread(grad_dt_bias, H, own_heads),
        spread(grad_a_log, H, own_heads),
        spread(grad_d_skip, H, own_heads),
        grad_norm_in,
        spread(grad_norm_out, inner, cols * group),
    ]
    sizes = [entry.shape[0] for entry in flat]
    packed = jnp.concatenate(flat)
    packed = jnp.pad(packed, (0, -packed.shape[0] % 1024)).reshape(-1, 128)
    packed = sum_axis(sum_axis(packed, STATE), DP).reshape(-1)
    summed = []
    at = 0
    for size in sizes:
        summed.append(packed[at : at + size])
        at += size
    return (
        block_out,
        grad_input,
        grad_in_proj,
        grad_out_proj,
        summed[0].reshape(CONV, xbc),
        summed[1],
        summed[2],
        summed[3],
        summed[4],
        summed[5],
        summed[6],
    )


def solution(mesh):
    rows = P((DP, STATE), None)
    whole = P()
    in_specs = (rows, P(DP), P(DP, STATE), P(STATE, DP)) + (whole,) * 7 + (rows,)
    out_specs = (rows, rows, P(DP, STATE), P(STATE, DP)) + (whole,) * 7

    return jax.shard_map(local, mesh=mesh, in_specs=in_specs, out_specs=out_specs, check_vma=False)
```

```python
import functools

import jax
import jax.numpy as jnp
from jax import lax
from jax.experimental import pallas as pl
from jax.experimental.pallas import tpu as pltpu
from jax.sharding import PartitionSpec as P

H = 64
P_SIZE = 64
N = 128
SPAN = 256
CONV = 4
EPSILON = 1e-05
F32 = jnp.float32
BF16 = jnp.bfloat16
DP, STATE = "dp", "state"
IN_ORDER = pltpu.CompilerParams(dimension_semantics=("arbitrary",))


def flip(value, axis, bit):
    return lax.ppermute(value, axis, [(i, i ^ bit) for i in range(lax.axis_size(axis))])


def moves(count, from_range, to_range):
    found = {}
    for source in range(count):
        for target in range(count):
            a, b = from_range(source), to_range(target)
            if source != target and max(a[0], b[0]) < min(a[1], b[1]):
                found.setdefault(target - source, []).append((source, target))
    return found


def stack_rows(parts, places):
    rows, width = parts[0].shape

    def kernel(places_ref, *refs):
        out = refs[-1]
        for i, part in enumerate(refs[:-1]):
            out[pl.ds(pl.multiple_of(places_ref[i] * rows, rows), rows), :] = part[...]

    return pl.pallas_call(
        kernel,
        in_specs=[pl.BlockSpec(memory_space=pltpu.SMEM)]
        + [pl.BlockSpec(memory_space=pltpu.VMEM) for _ in parts],
        out_specs=pl.BlockSpec(memory_space=pltpu.VMEM),
        out_shape=jax.ShapeDtypeStruct((rows * len(parts), width), parts[0].dtype),
    )(places, *parts)


def gather_state(own):
    count, here = lax.axis_size(STATE), lax.axis_index(STATE)
    held = {0: own}
    bit = count // 2
    while bit:
        for key in list(held):
            held[key | bit] = flip(held[key], STATE, bit)
        bit //= 2
    keys = sorted(held)
    return stack_rows([held[key] for key in keys], here ^ jnp.array(keys))


def ringed(axis):
    return lax.axis_size(axis) <= 8


def to_ring(value, axis):
    if not ringed(axis):
        return value
    count, here = lax.axis_size(axis), lax.axis_index(axis)
    steps = count // 2
    pair = value.shape[1] // count
    sides = []
    for side in range(2):
        blocks = [value[:, (2 * i + side) * pair : (2 * i + side + 1) * pair] for i in range(steps)][::-1]
        turned = jnp.concatenate(blocks + blocks[:-1], axis=1)
        sides.append(lax.dynamic_slice_in_dim(turned, (steps - 1 - here // 2) * pair, steps * pair, 1))
    even = here % 2 == 0
    return jnp.concatenate([jnp.where(even, *sides), jnp.where(even, *sides[::-1])], axis=1)


def from_ring(value, axis):
    if not ringed(axis):
        return value
    count, here = lax.axis_size(axis), lax.axis_index(axis)
    steps = count // 2
    pair = value.shape[1] // count
    first, second = value[:, : steps * pair], value[:, steps * pair :]
    even = here % 2 == 0
    sides = []
    for side in (jnp.where(even, first, second), jnp.where(even, second, first)):
        blocks = [side[:, i * pair : (i + 1) * pair] for i in range(steps)][::-1]
        turned = jnp.concatenate(blocks + blocks[:-1], axis=1)
        sides.append(lax.dynamic_slice_in_dim(turned, (steps - 1 - here // 2) * pair, steps * pair, 1))
    return jnp.concatenate(
        [sides[i % 2][:, i // 2 * pair : (i // 2 + 1) * pair] for i in range(count)], axis=1
    )


def gather_dp(own):
    count = lax.axis_size(DP)
    if not ringed(DP):
        return [lax.all_gather(own, DP, axis=1, tiled=True)]
    ring = [(i, (i + 2) % count) for i in range(count)]
    mine, other = [own], []
    for step in range(count // 2):
        other.append(flip(mine[step], DP, 1))
        if step + 1 < count // 2:
            mine.append(lax.ppermute(mine[step], DP, ring))
    return mine + other


def scatter_dp(products):
    count = lax.axis_size(DP)

    def multiply(left, some, kind):
        return lax.dot_general(left, some, (((0,), (0,)), ((), ())), preferred_element_type=kind)

    if not ringed(DP):
        return [
            lax.psum_scatter(multiply(left, right, F32), DP, scatter_dimension=1, tiled=True)
            for left, right, _ in products
        ]
    steps = count // 2
    half = products[0][1].shape[1] // 2
    wide = half // steps
    ring = [(i, (i + 2) % count) for i in range(count)]
    sides = []
    for left, right, label in products:
        other = multiply(left, right[:, half:], BF16)
        mine = multiply(left, right[:, :half], BF16)
        sides.append((mine, other, label))
    carried = None
    for step in range(1, steps + 1):
        at = step % steps * wide
        totals = []
        for mine, other, label in sides:
            came = flip(other[:, at : at + wide], DP, 1)
            totals.append(mine[:, at : at + wide].astype(F32) + came.astype(F32))
        if carried is not None:
            place = 0
            for i, total in enumerate(totals):
                totals[i] = total + carried[place : place + total.shape[0]].astype(F32)
                place += total.shape[0]
        if step < steps:
            joint = [total.astype(BF16) for total in totals]
            joint = jnp.concatenate(joint, axis=0) if len(joint) > 1 else joint[0]
            carried = lax.ppermute(joint, DP, ring)
    return totals


def scatter_state(whole):
    count, here = lax.axis_size(STATE), lax.axis_index(STATE)
    rows = whole.reshape(count, whole.shape[0] // count, whole.shape[1])
    parts = {key: lax.dynamic_index_in_dim(rows, here ^ key, 0, keepdims=False) for key in range(count)}
    bit = 1
    while bit < count:
        for key in [k for k in parts if not k & bit]:
            sent = flip(parts.pop(key | bit).astype(BF16), STATE, bit)
            parts[key] = parts[key].astype(F32) + sent.astype(F32)
        bit *= 2
    return parts[0]


def sum_axis(value, axis):
    bits = []
    while 1 << len(bits) < lax.axis_size(axis):
        bits.append(1 << len(bits))
    for bit in bits:
        value = value + flip(value, axis, bit)
    return value


def meet(first, second):
    low, high = max(first[0], second[0]), min(first[1], second[1])
    return (low, high) if low < high else None


def cut_rows(own, group, plans):
    groups = len(plans[0])
    store, width = own.shape
    sizes = [max(sum(b - a for a, b in ranges) for ranges in plan if ranges) for plan in plans]

    def kernel(group_ref, own_ref, *outs):
        for out in outs:
            out[...] = jnp.zeros_like(out)
        for g in range(groups):

            @pl.when(group_ref[0] == g)
            def _():
                for out, plan in zip(outs, plans):
                    at = 0
                    for ask in plan[g] or []:
                        found = meet(ask, (store * g, store * (g + 1)))
                        if found:
                            low, high = found
                            out[at + low - ask[0] : at + high - ask[0], :] = own_ref[low - store * g : high - store * g, :]
                        at += ask[1] - ask[0]

    return pl.pallas_call(
        kernel,
        in_specs=[pl.BlockSpec(memory_space=pltpu.SMEM), pl.BlockSpec(memory_space=pltpu.VMEM)],
        out_specs=[pl.BlockSpec(memory_space=pltpu.VMEM) for _ in plans],
        out_shape=[jax.ShapeDtypeStruct((size, width), BF16) for size in sizes],
        name="cut",
    )(group[None], own)


def paste_rows(pieces, group, plans, store):
    groups = len(plans[0])
    width = pieces[0].shape[1]

    def kernel(group_ref, *refs):
        out = refs[-1]
        out[...] = jnp.zeros_like(out)
        for g in range(groups):

            @pl.when(group_ref[0] == g)
            def _():
                for piece, plan in zip(refs[:-1], plans):
                    at = 0
                    for ask in plan[g] or []:
                        found = meet(ask, (store * g, store * (g + 1)))
                        if found:
                            low, high = found
                            out[low - store * g : high - store * g, :] += piece[
                                at + low - ask[0] : at + high - ask[0], :
                            ].astype(F32)
                        at += ask[1] - ask[0]

    return pl.pallas_call(
        kernel,
        in_specs=[pl.BlockSpec(memory_space=pltpu.SMEM)]
        + [pl.BlockSpec(memory_space=pltpu.VMEM) for _ in pieces],
        out_specs=pl.BlockSpec(memory_space=pltpu.VMEM),
        out_shape=jax.ShapeDtypeStruct((store, width), F32),
        name="paste",
    )(group[None], *pieces)


def spans(size):
    half = size // 2
    return [(0, half, half), (half, size, size)]


def dots(left, right, contract, exact=False):
    return lax.dot_general(
        left,
        right,
        (contract, ((), ())),
        preferred_element_type=F32,
        precision=lax.Precision.HIGHEST if exact else None,
    )


def softplus(value):
    return jnp.maximum(value, 0.0) + jnp.log1p(jnp.exp(-jnp.abs(value)))


def triangle(size, upper):
    row = lax.broadcasted_iota(jnp.int32, (size, size), 0)
    col = lax.broadcasted_iota(jnp.int32, (size, size), 1)
    return (row <= col if upper else row >= col).astype(F32)


def decays(raw, place, bias, bias_t, rate, rate_t):
    pre = dots(raw, place, ((1,), (1,))) + bias
    pre_t = dots(place, raw, ((1,), (1,))) + bias_t
    step, step_t = softplus(pre), softplus(pre_t)
    size = raw.shape[0]
    log = dots(triangle(size, False), step * rate, ((1,), (0,)), True)
    log_t = dots(step_t * rate_t, triangle(size, True), ((1,), (0,)), True)
    return pre, step, step_t, log, log_t


def decay_of(log, log_t, head, span):
    first, last, seen = span
    gap = log[first:last, head : head + 1] - log_t[head : head + 1, :seen]
    row = first + lax.broadcasted_iota(jnp.int32, gap.shape, 0)
    col = lax.broadcasted_iota(jnp.int32, gap.shape, 1)
    return jnp.exp(jnp.where(row >= col, gap, -jnp.inf))


def convolve(before, here, taps, bias):
    ext = jnp.concatenate([before, here], axis=0)
    size = here.shape[0]
    start = before.shape[0] - (CONV - 1)
    total = bias + taps[0:1] * ext[start : start + size]
    for offset in range(1, CONV):
        total = total + taps[offset : offset + 1] * ext[start + offset : start + offset + size]
    return total, ext


def join(pieces, whole):
    @pl.when(pl.program_id(0) == 0)
    def _():
        wide = pieces[0].shape[1]
        for i, piece in enumerate(pieces):
            whole[:, i * wide : (i + 1) * wide] = piece[...]


def joined(pieces):
    return pltpu.VMEM((pieces[0].shape[0], sum(p.shape[1] for p in pieces)), BF16)


def row_of_sums(value):
    total = value[:, :128]
    for at in range(128, value.shape[1], 128):
        total = total + value[:, at : at + 128]
    return dots(jnp.ones((8, 128), F32), total, ((1,), (1,)), True)


def scan_forward(is_first, *refs):
    x_ref, taps_ref, cbias_ref, place_ref, bias_ref, bias_t_ref, rate_ref, rate_t_ref, skip_ref = refs[:9]
    act_ref, mixed_ref, starts_ref, halo, state = refs[-5:]

    @pl.when(pl.program_id(0) == 0)
    def _():
        for new, old in zip((halo, state), refs[-7:-5]):
            new[...] = jnp.zeros_like(new) if is_first else old[...]

    size = x_ref.shape[0]
    heads = place_ref.shape[0]
    cols = heads * P_SIZE
    wide = cols + 2 * N
    for at in range(0, wide, 128):
        here = x_ref[:, at : at + 128].astype(F32)
        conv, _ = convolve(halo[:, at : at + 128], here, taps_ref[:, at : at + 128], cbias_ref[:, at : at + 128])
        act_ref[:, at : at + 128] = (conv * jax.nn.sigmoid(conv)).astype(BF16)
        halo[:, at : at + 128] = here[size - 8 :]
    _, step, step_t, log, log_t = decays(
        x_ref[:, wide:], place_ref[...], bias_ref[...], bias_t_ref[...], rate_ref[...], rate_t_ref[...]
    )
    growth = jnp.exp(log)
    tail = jnp.exp(log[size - 1 :] - log) * step
    inputs_b = act_ref[:, cols : cols + N]
    readout = act_ref[:, cols + N :]
    scores = dots(readout, inputs_b, ((1,), (1,)))
    left = lax.broadcasted_iota(jnp.int32, (size, 128), 1) < P_SIZE
    upper = lax.broadcasted_iota(jnp.int32, (128, 128), 0) < P_SIZE
    for pair in range(heads // 2):
        at = pair * 128
        a, b = 2 * pair, 2 * pair + 1
        vals = act_ref[:, at : at + 128]
        vals_f = vals.astype(F32)
        held = state[at : at + 128, :]
        starts_ref[at : at + 128, :] = held
        outer = dots(readout, held.astype(BF16), ((1,), (1,)))
        base = jnp.where(left, growth[:, a : a + 1], growth[:, b : b + 1]) * outer + skip_ref[:, at : at + 128] * vals_f
        split = [jnp.where(left, vals, 0), jnp.where(left, 0, vals)]
        for span in spans(size):
            first, last, seen = span
            total = base[first:last]
            for head, part in ((a, split[0]), (b, split[1])):
                mix = scores[first:last, :seen] * decay_of(log, log_t, head, span) * step_t[head : head + 1, :seen]
                total = total + dots(mix.astype(BF16), part[:seen], ((1,), (0,)))
            mixed_ref[first:last, at : at + 128] = total
        low = (vals_f * jnp.where(left, tail[:, a : a + 1], tail[:, b : b + 1])).astype(BF16)
        keep = jnp.where(upper, growth[size - 1 :, a : a + 1], growth[size - 1 :, b : b + 1])
        state[at : at + 128, :] = keep * held + dots(low, inputs_b, ((0,), (0,)))


def scan_backward(is_last, is_first, *refs):
    (
        x_ref, before_ref, act_ref, grad_ref, starts_ref,
        taps_ref, cbias_ref, place_ref, bias_ref, bias_t_ref, rate_ref, rate_t_ref, skip_ref,
    ) = refs[:13]
    olds = refs[13:-12]
    out_ref, *news = refs[-12:-6]
    by_col, by_row, tails, score_sum, in_grad, read_grad = refs[-6:]
    for i, new in enumerate(news):
        new[...] = jnp.zeros_like(new) if is_last else olds[i + 1][...]
    after, state, conv_ref, skip_grad_ref, head_ref = news
    size = x_ref.shape[0]
    heads = place_ref.shape[0]
    cols = heads * P_SIZE
    wide = cols + 2 * N
    place = place_ref[...]
    pre, step, step_t, log, log_t = decays(
        x_ref[:, wide:], place, bias_ref[...], bias_t_ref[...], rate_ref[...], rate_t_ref[...]
    )
    growth = jnp.exp(log)
    tail_exp = jnp.exp(log[size - 1 :] - log)
    tail = tail_exp * step
    inputs_b = act_ref[:, cols : cols + N]
    readout = act_ref[:, cols + N :]
    scores = dots(readout, inputs_b, ((1,), (1,)))
    left = lax.broadcasted_iota(jnp.int32, (size, 128), 1) < P_SIZE
    upper = lax.broadcasted_iota(jnp.int32, (128, 128), 0) < P_SIZE

    def through_conv(at, grad):
        here = x_ref[:, at : at + 128].astype(F32)
        before = before_ref[8:, at : at + 128].astype(F32)
        if is_first:
            before = jnp.zeros_like(before)
        taps = taps_ref[:, at : at + 128]
        conv, ext = convolve(before, here, taps, cbias_ref[:, at : at + 128])
        sig = jax.nn.sigmoid(conv)
        grad = grad * (sig * (1.0 + conv * (1.0 - sig)))
        start = 8 - (CONV - 1)
        rows = [jnp.sum(grad * ext[start + o : start + o + size], axis=0, keepdims=True) for o in range(CONV)]
        rows += [jnp.sum(grad, axis=0, keepdims=True), jnp.zeros((3, 128), F32)]
        conv_ref[:, at : at + 128] += jnp.concatenate(rows, axis=0)
        onward = jnp.concatenate([grad, after[:, at : at + 128]], axis=0)
        after[:, at : at + 128] = grad[:8]
        total = taps[CONV - 1 : CONV] * grad
        for o in range(CONV - 1):
            total = total + taps[o : o + 1] * onward[CONV - 1 - o : CONV - 1 - o + size]
        out_ref[:, at : at + 128] = total.astype(BF16)

    score_sum[...] = jnp.zeros_like(score_sum)
    in_grad[...] = jnp.zeros_like(in_grad)
    read_grad[...] = jnp.zeros_like(read_grad)
    for pair in range(heads // 2):
        at = pair * 128
        a, b = 2 * pair, 2 * pair + 1
        vals = act_ref[:, at : at + 128]
        vals_f = vals.astype(F32)
        grad = grad_ref[:, at : at + 128]
        grad_f = grad.astype(F32)
        starts = starts_ref[at : at + 128, :]
        starts_low = starts.astype(BF16)
        held = state[at : at + 128, :]
        held_low = held.astype(BF16)
        grown = grad_f * jnp.where(left, growth[:, a : a + 1], growth[:, b : b + 1])
        outer_low = grown.astype(BF16)
        outer = grown * dots(readout, starts_low, ((1,), (1,)))
        read_grad[...] += dots(outer_low, starts_low, ((1,), (0,)))
        tail_pair = jnp.where(left, tail[:, a : a + 1], tail[:, b : b + 1])
        low = (vals_f * tail_pair).astype(BF16)
        in_grad[...] += dots(low, held_low, ((1,), (0,)))
        low_grad = dots(inputs_b, held_low, ((1,), (1,)))
        tail_part = low_grad * vals_f
        product = grad_f * vals_f
        skip_grad_ref[:, at : at + 128] += jnp.sum(product, axis=0, keepdims=True)
        keep = jnp.where(upper, growth[size - 1 :, a : a + 1], growth[size - 1 :, b : b + 1])
        shared = jnp.sum(held * starts, axis=1, keepdims=True)
        state[at : at + 128, :] = dots(outer_low, readout, ((0,), (0,))) + keep * held
        base = skip_ref[:, at : at + 128] * grad_f + low_grad * tail_pair
        top = base[: size // 2]
        bottom = base[size // 2 :]
        for head, side in ((a, left), (b, jnp.logical_not(left))):
            own = jnp.where(side, grad, 0)
            tails[:, head : head + 1] = jnp.sum(jnp.where(side, tail_part, 0.0), axis=1, keepdims=True)
            rows = []
            sums = jnp.zeros((1, size), F32)
            for span in spans(size):
                first, last, seen = span
                mix_grad = dots(own[first:last], vals[:seen], ((1,), (1,)))
                decay = decay_of(log, log_t, head, span)
                steps = step_t[head : head + 1, :seen]
                some = scores[first:last, :seen]
                decayed = mix_grad * decay
                by_score = decayed * some
                score_sum[first:last, :seen] += decayed * steps
                rows.append(jnp.sum(by_score * steps, axis=1, keepdims=True))
                sums = sums + jnp.pad(jnp.sum(by_score, axis=0, keepdims=True), ((0, 0), (0, size - seen)))
                back = dots((some * decay * steps).astype(BF16), own[first:last], ((0,), (0,)))
                top = top + back[: size // 2]
                if seen == size:
                    bottom = bottom + back[size // 2 :]
            by_row[head : head + 1, :] = sums
            flow = jnp.sum(jnp.where(side, outer, 0.0), axis=1, keepdims=True)
            by_col[:, head : head + 1] = jnp.concatenate(rows, axis=0) + flow
            half = shared[:P_SIZE] if head == a else shared[P_SIZE:]
            by_col[size - 1 :, head : head + 1] += growth[size - 1 :, head : head + 1] * jnp.sum(
                half, axis=0, keepdims=True
            )
        through_conv(at, jnp.concatenate([top, bottom], axis=0))

    score_grad = score_sum[...].astype(BF16)
    through_conv(cols, in_grad[...] + dots(score_grad, readout, ((0,), (0,))))
    through_conv(cols + N, read_grad[...] + dots(score_grad, inputs_b, ((1,), (0,))))

    eye = (
        lax.broadcasted_iota(jnp.int32, (heads, heads), 0) == lax.broadcasted_iota(jnp.int32, (heads, heads), 1)
    ).astype(F32)
    summed = dots(by_row[...], eye, ((0,), (0,)), True)
    tail_grad = tails[...]
    tail_term = tail_grad * tail
    log_grad = by_col[...] - step * summed - tail_term
    row = lax.broadcasted_iota(jnp.int32, log_grad.shape, 0)
    log_grad = log_grad + jnp.where(row == size - 1, jnp.sum(tail_term, axis=0, keepdims=True), 0.0)
    decay_grad = dots(triangle(size, True), log_grad, ((1,), (0,)), True)
    step_grad = summed + tail_grad * tail_exp + decay_grad * rate_ref[...]
    raw = step_grad * jax.nn.sigmoid(pre)
    head_ref[...] += jnp.concatenate(
        [
            jnp.sum(raw, axis=0, keepdims=True),
            jnp.sum(decay_grad * step, axis=0, keepdims=True) * rate_ref[...],
            jnp.zeros((6, heads), F32),
        ],
        axis=0,
    )
    out_ref[:, wide:] = dots(raw.astype(BF16), place, ((1,), (0,))).astype(BF16)


def whole_spec(value):
    return pl.BlockSpec(value.shape, lambda k: (0,) * value.ndim)


def row_spec(value):
    return pl.BlockSpec((SPAN, value.shape[1]), lambda k: (k, 0))


def project_kernel(left_ref, *refs):
    *pieces, out_ref, whole = refs
    join(pieces, whole)
    out_ref[...] = dots(left_ref[...], whole[...], ((1,), (1,))).astype(BF16)


def run_project(left, pieces):
    out = jax.ShapeDtypeStruct((left.shape[0], pieces[0].shape[0]), BF16)
    return pl.pallas_call(
        project_kernel,
        grid=(left.shape[0] // TALL,),
        in_specs=[tall_spec(left)] + [whole_spec(p) for p in pieces],
        out_specs=tall_spec(out),
        out_shape=out,
        scratch_shapes=[joined(pieces)],
        compiler_params=IN_ORDER,
        name="pj",
    )(left, *pieces)


def run_scan_forward(x_proj, params):
    rows, width = x_proj.shape
    wide = params[0].shape[1]
    cols = wide - 2 * N
    blocks = rows // SPAN
    per = 2
    outs = [
        jax.ShapeDtypeStruct((rows, wide), BF16),
        jax.ShapeDtypeStruct((rows, cols), F32),
        jax.ShapeDtypeStruct((blocks * cols, N), F32),
    ]
    carried = [jax.ShapeDtypeStruct((8, wide), F32), jax.ShapeDtypeStruct((cols, N), F32)]
    held = None
    for at in range(0, blocks, per):
        args = [x_proj, *params]
        ins = [pl.BlockSpec((SPAN, width), lambda k, at=at: (at + k, 0))] + [whole_spec(p) for p in params]
        aliases = {}
        if held is not None:
            aliases = {len(args) + i: i for i in range(len(held))}
            ins += [pl.BlockSpec(memory_space=pl.ANY) for _ in outs] + [whole_spec(c) for c in carried]
            args += held
        held = pl.pallas_call(
            functools.partial(scan_forward, held is None),
            grid=(per,),
            in_specs=ins,
            out_specs=[
                pl.BlockSpec((SPAN, wide), lambda k, at=at: (at + k, 0)),
                pl.BlockSpec((SPAN, cols), lambda k, at=at: (at + k, 0)),
                pl.BlockSpec((cols, N), lambda k, at=at: (at + k, 0)),
            ]
            + [whole_spec(c) for c in carried],
            out_shape=outs + carried,
            input_output_aliases=aliases,
            compiler_params=IN_ORDER,
        )(*args)
    return held[:3]


TALL = 2 * SPAN


def tall_spec(value):
    return pl.BlockSpec((TALL, value.shape[1]), lambda k: (k, 0))


def across_spec():
    return pl.BlockSpec((8, TALL), lambda k: (0, k))


def gate_kernel(*refs):
    normed_ref, mixed_ref, mask_ref, *pieces, gate_ref, square_ref, whole = refs
    join(pieces, whole)
    gate = dots(normed_ref[...], whole[...], ((1,), (1,))).astype(BF16)
    gate_ref[...] = gate
    gate = gate.astype(F32)
    gated = mixed_ref[...] * (gate * jax.nn.sigmoid(gate)) * mask_ref[...]
    square_ref[...] = row_of_sums(gated * gated)


def run_gate(normed, mixed, mask, pieces):
    rows, cols = mixed.shape
    return pl.pallas_call(
        gate_kernel,
        grid=(rows // TALL,),
        in_specs=[tall_spec(normed), tall_spec(mixed), whole_spec(mask)] + [whole_spec(p) for p in pieces],
        out_specs=[tall_spec(mixed), across_spec()],
        out_shape=[jax.ShapeDtypeStruct((rows, cols), BF16), jax.ShapeDtypeStruct((8, rows), F32)],
        scratch_shapes=[joined(pieces)],
        compiler_params=IN_ORDER,
        name="gf",
    )(normed, mixed, mask, *pieces)


def normalize_kernel(mixed_ref, gate_ref, scale_ref, gain_ref, out_ref):
    gate = gate_ref[...].astype(F32)
    gated = mixed_ref[...] * (gate * jax.nn.sigmoid(gate))
    out_ref[...] = (gated * scale_ref[...] * gain_ref[...]).astype(BF16)


def run_normalize(mixed, gate, scale, gain):
    return pl.pallas_call(
        normalize_kernel,
        grid=(mixed.shape[0] // SPAN,),
        in_specs=[row_spec(mixed), row_spec(gate), row_spec(scale), whole_spec(gain)],
        out_specs=row_spec(gate),
        out_shape=jax.ShapeDtypeStruct(gate.shape, BF16),
        name="nr",
    )(mixed, gate, scale, gain)


def gate_grad_kernel(*refs):
    cot_ref, mixed_ref, gate_ref, scale_ref, gain_ref, mask_ref, *pieces, grad_ref, aligned_ref, norm_ref, whole = refs
    join(pieces, whole)
    grad = dots(cot_ref[...], whole[...], ((1,), (1,)))
    grad_ref[...] = grad
    gate = gate_ref[...].astype(F32)
    product = grad * (mixed_ref[...] * (gate * jax.nn.sigmoid(gate)) * mask_ref[...])
    aligned_ref[...] = row_of_sums(product * gain_ref[...])

    @pl.when(pl.program_id(0) == 0)
    def _():
        norm_ref[...] = jnp.zeros_like(norm_ref)

    norm_ref[...] += jnp.sum(product * scale_ref[...], axis=0, keepdims=True)


def run_gate_grad(cot, mixed, gate, scale, gain, mask, pieces):
    rows, cols = mixed.shape
    return pl.pallas_call(
        gate_grad_kernel,
        grid=(rows // TALL,),
        in_specs=[tall_spec(cot), tall_spec(mixed), tall_spec(gate), tall_spec(scale)]
        + [whole_spec(gain), whole_spec(mask)]
        + [whole_spec(p) for p in pieces],
        out_specs=[tall_spec(mixed), across_spec(), pl.BlockSpec((1, cols), lambda k: (0, 0))],
        out_shape=[
            jax.ShapeDtypeStruct((rows, cols), F32),
            jax.ShapeDtypeStruct((8, rows), F32),
            jax.ShapeDtypeStruct((1, cols), F32),
        ],
        scratch_shapes=[joined(pieces)],
        compiler_params=IN_ORDER,
        name="gb",
    )(cot, mixed, gate, scale, gain, mask, *pieces)


def run_products(left, pieces, onto=None, against=None):
    rows = left.shape[0]
    others = [] if onto is None else [onto, against]

    def kernel(left_ref, *refs):
        join(refs[: len(pieces)], refs[-1])
        total = dots(left_ref[...], refs[-1][...], ((1,), (0,)))
        if others:
            onto_ref, against_ref, out_ref, sums_ref = refs[len(pieces) : -1]
            total = total + onto_ref[...].astype(F32)
            sums = jnp.sum(total * against_ref[...].astype(F32), axis=0, keepdims=True)

            @pl.when(pl.program_id(0) == 0)
            def _():
                sums_ref[...] = sums

            @pl.when(pl.program_id(0) > 0)
            def _():
                sums_ref[...] += sums

        else:
            out_ref = refs[-2]
        out_ref[...] = total.astype(BF16)

    whole = joined(pieces)
    out = jax.ShapeDtypeStruct((rows, whole.shape[1]), BF16)
    sums = [jax.ShapeDtypeStruct((1, whole.shape[1]), F32)] if others else []
    return pl.pallas_call(
        kernel,
        grid=(rows // TALL,),
        in_specs=[tall_spec(left)] + [whole_spec(p) for p in pieces] + [tall_spec(o) for o in others],
        out_specs=[tall_spec(out)] + [whole_spec(total) for total in sums],
        out_shape=[out] + sums,
        scratch_shapes=[whole],
        compiler_params=IN_ORDER,
    )(left, *pieces, *others)


def run_scan_backward(x_proj, act, mixed_low, starts, params):
    rows, width = x_proj.shape
    wide = act.shape[1]
    cols = wide - 2 * N
    heads = cols // P_SIZE
    blocks = rows // SPAN
    carried = [
        jax.ShapeDtypeStruct((8, wide), F32),
        jax.ShapeDtypeStruct((cols, N), F32),
        jax.ShapeDtypeStruct((8, wide), F32),
        jax.ShapeDtypeStruct((1, cols), F32),
        jax.ShapeDtypeStruct((8, heads), F32),
    ]
    held = None
    for at in range(blocks - 1, -1, -1):
        ins = [
            pl.BlockSpec((SPAN, width), lambda k, at=at: (at, 0)),
            pl.BlockSpec((16, width), lambda k, at=at: (max(at * (SPAN // 16) - 1, 0), 0)),
            pl.BlockSpec((SPAN, wide), lambda k, at=at: (at, 0)),
            pl.BlockSpec((SPAN, cols), lambda k, at=at: (at, 0)),
            pl.BlockSpec((cols, N), lambda k, at=at: (at, 0)),
        ] + [whole_spec(p) for p in params]
        args = [x_proj, x_proj, act, mixed_low, starts, *params]
        aliases = {}
        if held is not None:
            aliases = {len(args) + i: i for i in range(len(held))}
            ins += [pl.BlockSpec(memory_space=pl.ANY)] + [whole_spec(c) for c in carried]
            args += held
        held = pl.pallas_call(
            functools.partial(scan_backward, held is None, at == 0),
            grid=(1,),
            in_specs=ins,
            out_specs=[pl.BlockSpec((SPAN, width), lambda k, at=at: (at, 0))] + [whole_spec(c) for c in carried],
            out_shape=[jax.ShapeDtypeStruct((rows, width), BF16)] + carried,
            input_output_aliases=aliases,
            scratch_shapes=[
                pltpu.VMEM((SPAN, heads), F32),
                pltpu.VMEM((heads, SPAN), F32),
                pltpu.VMEM((SPAN, heads), F32),
                pltpu.VMEM((SPAN, SPAN), F32),
                pltpu.VMEM((SPAN, N), F32),
                pltpu.VMEM((SPAN, N), F32),
            ],
        )(*args)
    return held[0], *held[3:]


def local(
    block_input,
    width_index,
    w_in,
    w_out,
    conv_weight,
    conv_bias,
    dt_bias,
    a_log,
    d_skip,
    norm_in_gain,
    norm_out_gain,
    out_cotangent,
):
    tok_rows, _ = block_input.shape
    inner = H * P_SIZE
    xbc = inner + 2 * N
    full_cols = 2 * inner + 2 * N + H
    groups, group = lax.axis_size(STATE), lax.axis_index(STATE)
    seq_rows = tok_rows * groups
    heads = H // groups
    cols = inner // groups
    store = full_cols // groups

    def store_range(i):
        return (store * i, store * (i + 1))

    def value_range(i):
        return (inner + cols * i, inner + cols * (i + 1))

    def gate_range(i):
        return (cols * i, cols * (i + 1))

    def tail_range(i):
        return (inner + inner, full_cols)

    value_moves = moves(groups, store_range, value_range)
    tail_moves = moves(groups, store_range, tail_range)
    gate_moves = moves(groups, store_range, gate_range)

    def x_ranges(i):
        return [value_range(i), tail_range(i)]

    def at_shift(ranges, shift):
        return [ranges(g + shift) if 0 <= g + shift < groups else None for g in range(groups)]

    kinds = (("v", value_range, value_moves), ("b", tail_range, tail_moves), ("g", gate_range, gate_moves))
    sends = [(kind + str(abs(shift)), ranges, shift, found[shift]) for kind, ranges, found in kinds for shift in sorted(found)]
    plans = [at_shift(x_ranges, 0), at_shift(lambda i: [gate_range(i)], 0)]
    plans += [at_shift(lambda i, ranges=ranges: [ranges(i)], shift) for _, ranges, shift, _ in sends]
    w_x_own, w_g_own, *cuts = cut_rows(w_in.T, group, plans)
    came = {"v": None, "b": None, "g": None}
    for (name, _, _, found), cut in zip(sends, cuts):
        part = lax.ppermute(cut, STATE, found)
        came[name[0]] = part if came[name[0]] is None else came[name[0]] + part
    w_x_own = w_x_own + jnp.concatenate([came["v"], came["b"]], axis=0)
    w_g_own = w_g_own + came["g"]

    tokens = block_input.astype(F32)
    in_scale = lax.rsqrt(jnp.mean(tokens * tokens, axis=-1, keepdims=True) + EPSILON)
    normed = (tokens * in_scale * norm_in_gain).astype(BF16)

    w_x = gather_dp(w_x_own)
    normed_all = gather_state(to_ring(normed, DP))
    w_g = gather_dp(w_g_own)
    cot_all = gather_state(to_ring(out_cotangent, DP))
    w_o = gather_dp(w_out)

    own_heads = heads * group

    def own(entries, at, size):
        return lax.dynamic_slice_in_dim(entries, at, size, entries.ndim - 1)

    taps = jnp.concatenate([own(conv_weight, cols * group, cols), conv_weight[:, inner:]], axis=1)
    bias = jnp.concatenate([own(conv_bias, cols * group, cols), conv_bias[inner:]], axis=0)[None]
    gain_own = own(norm_out_gain, cols * group, cols)
    dt_own = own(dt_bias, own_heads, heads)
    rate_own = -jnp.exp(own(a_log, own_heads, heads))
    skip_own = jnp.repeat(own(d_skip, own_heads, heads), P_SIZE)[None]
    place = (own_heads + jnp.arange(heads)[:, None] == jnp.arange(H)[None, :]).astype(BF16)
    scan_params = (taps, bias, place, dt_own[None], dt_own[:, None], rate_own[None], rate_own[:, None], skip_own)
    x_proj = run_project(normed_all, w_x)
    act, mixed, starts = run_scan_forward(x_proj, scan_params)

    heads_on = H // 8 * jnp.left_shift(1, width_index[0])
    mask = ((cols * group + jnp.arange(cols)) // P_SIZE < heads_on).astype(F32)[None]
    active = (heads_on * P_SIZE).astype(F32)
    gain_mask = gain_own[None] * mask
    gate, square = run_gate(normed_all, mixed, mask, w_g)
    square = lax.psum(square[:1], STATE)
    scale_row = lax.rsqrt(square / active + EPSILON)
    out_scale = scale_row.reshape(seq_rows, 1)
    normed_out = run_normalize(mixed, gate, out_scale, gain_mask)

    out_grad, aligned, norm_sums = run_gate_grad(cot_all, mixed, gate, out_scale, gain_mask, mask, w_o)
    grad_norm_out = norm_sums[0]
    mixed, gate, out_grad = lax.optimization_barrier((mixed, gate, out_grad))
    gate_f = gate.astype(F32)
    gate_sig = jax.nn.sigmoid(gate_f)
    gate_act = gate_f * gate_sig
    gated = mixed * gate_act
    aligned = lax.psum(aligned[:1], STATE).reshape(seq_rows, 1)
    pull = (aligned / active) * out_scale * out_scale * out_scale
    gated_grad = out_grad * gain_mask * out_scale - gated * mask * pull
    mixed_grad = gated_grad * gate_act
    gate_grad = (gated_grad * mixed * (gate_sig * (1.0 + gate_f * (1.0 - gate_sig)))).astype(BF16)

    (out_whole,) = run_products(normed_out, w_o)
    block_out = (tokens + from_ring(scatter_state(out_whole), DP)).astype(BF16)
    grad_out_proj, grad_in_gate = scatter_dp([(normed_out, cot_all, "o"), (gate_grad, normed_all, "g")])
    x_grad, conv_sums, skip_sums, head_sums = run_scan_backward(
        x_proj, act, mixed_grad.astype(BF16), starts, scan_params
    )
    taps_cols, bias_cols = conv_sums[:CONV], conv_sums[CONV]
    grad_d_skip = jnp.sum(skip_sums.reshape(heads, P_SIZE), axis=1)
    grad_dt_bias, grad_a_log = head_sums[0], head_sums[1]

    (grad_in_x,) = scatter_dp([(x_grad, normed_all, "x")])
    x_low, gate_low = grad_in_x.astype(BF16), grad_in_gate.astype(BF16)
    held = {"v": x_low[:cols], "b": x_low[cols:], "g": gate_low}
    pieces = [grad_in_x, grad_in_gate]
    plans = [at_shift(x_ranges, 0), at_shift(lambda i: [gate_range(i)], 0)]
    for name, ranges, shift, found in sends:
        pieces.append(lax.ppermute(held[name[0]], STATE, [(b, a) for a, b in found]))
        plans.append(at_shift(lambda i, ranges=ranges: [ranges(i)], shift))
    grad_in_proj = paste_rows(pieces, group, plans, store).T

    (normed_x,) = run_products(x_grad, w_x)
    normed_whole, gain_sums = run_products(gate_grad, w_g, normed_x, normed_all)
    normed_grad = from_ring(scatter_state(normed_whole), DP)
    pushed = normed_grad * norm_in_gain
    token_grad = in_scale * pushed - tokens * (
        in_scale * in_scale * in_scale * jnp.mean(pushed * tokens, axis=-1, keepdims=True)
    )
    grad_input = out_cotangent.astype(F32) + token_grad
    grad_norm_in = from_ring(gain_sums, DP)[0] / norm_in_gain

    def spread(entries, total, at):
        return lax.dynamic_update_slice_in_dim(
            jnp.zeros(entries.shape[:-1] + (total,), F32), entries, at, entries.ndim - 1
        )

    taps_wide = spread(taps_cols[:, :cols], xbc, cols * group).at[:, inner:].set(taps_cols[:, cols:])
    bias_wide = spread(bias_cols[:cols], xbc, cols * group).at[inner:].set(bias_cols[cols:])
    flat = [
        taps_wide.reshape(-1),
        bias_wide,
        spread(grad_dt_bias, H, own_heads),
        spread(grad_a_log, H, own_heads),
        spread(grad_d_skip, H, own_heads),
        grad_norm_in,
        spread(grad_norm_out, inner, cols * group),
    ]
    sizes = [entry.shape[0] for entry in flat]
    packed = jnp.concatenate(flat)
    packed = jnp.pad(packed, (0, -packed.shape[0] % 1024)).reshape(-1, 128)
    packed = sum_axis(sum_axis(packed, STATE), DP).reshape(-1)
    summed = []
    at = 0
    for size in sizes:
        summed.append(packed[at : at + size])
        at += size
    return (
        block_out,
        grad_input,
        grad_in_proj,
        grad_out_proj,
        summed[0].reshape(CONV, xbc),
        summed[1],
        summed[2],
        summed[3],
        summed[4],
        summed[5],
        summed[6],
    )


def solution(mesh):
    rows = P((DP, STATE), None)
    whole = P()
    in_specs = (rows, P(DP), P(DP, STATE), P(STATE, DP)) + (whole,) * 7 + (rows,)
    out_specs = (rows, rows, P(DP, STATE), P(STATE, DP)) + (whole,) * 7

    return jax.shard_map(local, mesh=mesh, in_specs=in_specs, out_specs=out_specs, check_vma=False)
```
